128 devices in a mesh: row: 16 (over z, x), col: 8 (over y, core).
Axes of the slice: x: 4, y: 4, z: 4, core: 2. Of those that a mesh axis runs over, the one named last changes fastest.
Arguments:
- diag_block: float32 [512, 512], replicated, may hold values from 0 to 21.885, as said below
- panel: float32 [32768, 512], P('row'), may hold values from -6 to 6
- block_mask: int32 [128, 2], replicated, may hold values 0 or 1
- slab: float32 [32768, 8192], P('row', 'col'), may hold values from -6 to 6
Outputs:
- factor_rows: float32 [32768, 512], P('row')
- updated: float32 [32768, 8192], P('row', 'col')
- growth: float32 [], replicated
The draws below stay inside these ranges and needn't reach their ends.
Inputs may be any that keep to these rules, and one draw needn't show every extreme that they name: `diag_block`: symmetric; each diagonal entry exceeds the sum of the magnitudes of the other entries of its row by 1 or more.
All inputs are finite; a program needn't handle non-finite values.
Results may differ from the reference program's by a relative error of at most 0.000064.
Values sent between devices are 32-bit elements; how exact they have to be, the bound alone decides.
A program may use at most 128 MiB of HBM per device.

```python
import jax
import jax.numpy as jnp
from jax import lax

B = 256
PW = 512
TRAIL = 32768
SC = 8192
NBT = 128


def draw_diag_block(key, part):
    first_key, second_key = jax.random.split(jax.random.fold_in(key, 11))
    margin = jax.random.uniform(second_key, (PW,), jnp.float32, 1.0, 2.0)
    raw = jax.random.uniform(first_key, (PW, PW), jnp.float32, 0.0, 0.035)
    eye = jnp.eye(PW, dtype=jnp.float32)
    sym = (raw + raw.T) * 0.5 * (1.0 - eye)
    row_total = jnp.sum(sym, axis=1)
    return sym + eye * (row_total + margin)


def with_ends(entries, key, smallest, largest):
    spot = [jax.random.randint(jax.random.fold_in(key, axis), (), 0, length) for axis, length in enumerate(entries.shape)]
    main_axis = entries.shape.index(max(entries.shape))
    next_to = spot[:main_axis] + [(spot[main_axis] + 1) % entries.shape[main_axis]] + spot[main_axis + 1:]
    return entries.at[tuple(spot)].set(smallest).at[tuple(next_to)].set(largest)


def steps_of(rng, extent, pieces, smallest, high):
    level, own = 1.0, jax.random.fold_in(rng, 6)
    for axis_at, shards_of in pieces:
        steps = jnp.exp(jax.random.uniform(jax.random.fold_in(own, axis_at), (shards_of,), jnp.float32, smallest / len(pieces), high / len(pieces)))
        level = level * jnp.repeat(steps, extent[axis_at] // shards_of).reshape([-1 if axis == axis_at else 1 for axis in range(len(extent))])
    return level


def centred(key, shape, deviation, most, pieces=(), kind=jnp.bfloat16):
    array = jax.random.normal(key, shape, jnp.float32) * deviation
    if len(pieces) > 0:
        array = steps_of(key, shape, pieces, -0.22, 0.18) * array
    return jnp.clip(array, min=-most, max=most).astype(kind)


def setup_inputs(seed: int = 0) -> dict:
    seeds = jax.random.split(jax.random.key(seed), 5)
    return {
        "diag_block": draw_diag_block(jax.random.fold_in(seeds[4], 71), 0),
        "panel": centred(seeds[1], (TRAIL, PW), 1.0, 6.0, ((0, 16),), jnp.float32),
        "block_mask": with_ends((jax.random.randint(seeds[2], (NBT, 2), 0, 4) < 3).astype(jnp.int32), jax.random.fold_in(seeds[2], 1), 0, 1),
        "slab": centred(seeds[3], (TRAIL, SC), 1.0, 6.0, ((0, 16), (1, 8)), jnp.float32),
    }


def right_solve(lower_factor, rows):
    return lax.linalg.triangular_solve(lower_factor, rows, left_side=False, lower=True, transpose_a=True)

def factor_diag(diag_block):
    top = jnp.linalg.cholesky(diag_block[:B, :B])
    link = right_solve(top, diag_block[B:, :B])
    rest = diag_block[B:, B:] - jnp.dot(link, link.T, precision=lax.Precision.HIGHEST)
    bottom = jnp.linalg.cholesky(rest)
    return (top, link, bottom)

def solve_rows(masked, top, link, bottom):
    first = right_solve(top, masked[:, :B])
    rest = masked[:, B:] - jnp.dot(first, link.T, precision=lax.Precision.HIGHEST)
    second = right_solve(bottom, rest)
    return jnp.concatenate([first, second], axis=1)

def reference(diag_block, panel, block_mask, slab):
    expanded = jnp.repeat(jnp.repeat(block_mask, B, axis=0), B, axis=1)
    masked = panel * expanded.astype(jnp.float32)
    top, link, bottom = factor_diag(diag_block)
    factor_rows = solve_rows(masked, top, link, bottom)
    updated = slab - jnp.dot(factor_rows, factor_rows[:SC].T, precision=lax.Precision.HIGHEST)
    growth = jnp.max(jnp.abs(updated))
    return (factor_rows, updated, growth)
```

```python
import jax
import jax.numpy as jnp
from jax import lax
from jax.experimental import pallas as pl
from jax.experimental.pallas import tpu as pltpu
from jax.sharding import PartitionSpec as P

B = 256
PW = 512
COARSE = 7
FINE = 3
MESH = pl.DeviceIdType.MESH
f32 = jnp.float32
bf16 = jnp.bfloat16


def nn(a, b):
    return lax.dot_general(a, b, (((1,), (0,)), ((), ())), preferred_element_type=f32)


def nt(a, b):
    return lax.dot_general(a, b, (((1,), (1,)), ((), ())), preferred_element_type=f32)


def split(a):
    high = a.astype(bf16)
    return high, (a - high.astype(f32)).astype(bf16)


def nt3(ah, al, bh, bl):
    return nt(ah, bh) + (nt(ah, bl) + nt(al, bh))


def nn3(ah, al, bh, bl):
    return nn(ah, bh) + (nn(ah, bl) + nn(al, bh))


def rows_at(start, size):
    return pl.ds(pl.multiple_of(start, 16), size)


def front_kernel(
    diag_ref, mask_ref, panel_ref, rows_ref, ch_ref, cl_ref,
    ah, al, w, wh, wl, mine, need,
    panel_sem, rows_sem, self_sem, out_sem, in_sem, ring_send, ring_recv,
):
    row, col = lax.axis_index("row"), lax.axis_index("col")
    z, x = row // 4, row % 4
    y, core = col // 2, col % 2
    right, left = z * 4 + (x + 1) % 4, z * 4 + (x + 3) % 4
    up, down = ((z + 1) % 4) * 4 + x, ((z + 3) % 4) * 4 + x
    half = need.shape[0] // 2
    piece = half // 16

    is_source = row < 4
    is_self = jnp.logical_and(row == 0, y == 0)
    source = (y, z * 2 + core)

    def spot(which, dz, dx):
        if which == 0:
            return (dz * 4 + dx) * piece
        return half + (dx * 4 + dz) * piece

    def scatter(which, dx):
        start = spot(which, y, dx)
        return (
            panel_ref.at[rows_at(core * 2 * half + start, piece)],
            need.at[rows_at(start, piece)],
            (y * 4 + dx, row * 2 + core),
        )

    barrier = pltpu.get_barrier_semaphore()

    def greet(device):
        pl.semaphore_signal(barrier, inc=1, device_id=device, device_id_type=MESH)

    for other in (right, left, up, down):
        greet((other, col))

    @pl.when(jnp.logical_not(is_self))
    def _():
        greet(source)

    @pl.when(is_source)
    def _():
        for dx in range(1, 4):
            greet((y * 4 + dx, row * 2 + core))

    @pl.when(jnp.logical_and(is_source, jnp.logical_not(is_self)))
    def _():
        greet((y * 4, row * 2 + core))

    others = 1 - is_self.astype(jnp.int32)
    pl.semaphore_wait(barrier, 4 + others + jnp.where(is_source, 3 + others, 0))

    def remote(which, dx):
        src, dst, device = scatter(which, dx)
        return pltpu.make_async_remote_copy(
            src_ref=src, dst_ref=dst, send_sem=out_sem.at[which * 4 + dx], recv_sem=in_sem.at[which],
            device_id=device, device_id_type=MESH,
        )

    def own(which):
        src, dst, _ = scatter(which, 0)
        return pltpu.make_async_copy(src, dst, self_sem.at[which])

    @pl.when(is_source)
    def _():
        for dx in range(1, 4):
            for which in range(2):
                remote(which, dx).start()

    @pl.when(jnp.logical_and(is_source, jnp.logical_not(is_self)))
    def _():
        for which in range(2):
            remote(which, 0).start()

    @pl.when(is_self)
    def _():
        for which in range(2):
            own(which).start()

    fetch = pltpu.make_async_copy(panel_ref, mine, panel_sem)
    fetch.start()

    def hop(index, start, size, device):
        part = need.at[rows_at(start, size)]
        return pltpu.make_async_remote_copy(
            src_ref=part, dst_ref=part, send_sem=ring_send.at[index], recv_sem=ring_recv.at[index],
            device_id=(device, col), device_id_type=MESH,
        )

    lx, rx, dz, uz = (x + 3) % 4, (x + 1) % 4, (z + 3) % 4, (z + 1) % 4

    def sends(step):
        wide = piece * 4
        if step == 0:
            return [
                hop(0, spot(0, z, x), piece, right), hop(1, spot(0, z, x), piece, left),
                hop(2, spot(1, z, x), piece, up), hop(3, spot(1, z, x), piece, down),
            ]
        if step == 1:
            part = piece // 2
            return [
                hop(4, spot(0, z, lx), part, right), hop(5, spot(0, z, rx) + part, part, left),
                hop(6, spot(1, dz, x), part, up), hop(7, spot(1, uz, x) + part, part, down),
            ]
        if step == 2:
            return [
                hop(8, z * wide, wide, up), hop(9, z * wide, wide, down),
                hop(10, half + x * wide, wide, right), hop(11, half + x * wide, wide, left),
            ]
        part = wide // 2
        return [
            hop(12, dz * wide, part, up), hop(13, uz * wide + part, part, down),
            hop(14, half + lx * wide, part, right), hop(15, half + rx * wide + part, part, left),
        ]

    def launch(step):
        for copy in sends(step):
            copy.start()

    def arrive(step):
        for copy in sends(step):
            copy.wait_recv()

    a = diag_ref[...]
    r_id = lax.broadcasted_iota(jnp.int32, (PW, PW), 0)
    c_id = lax.broadcasted_iota(jnp.int32, (PW, PW), 1)
    on_diag = jnp.where(r_id == c_id, a, 0.0)
    scale_rows = lax.rsqrt(jnp.sum(on_diag, axis=1, keepdims=True))
    scale_cols = lax.rsqrt(jnp.sum(on_diag, axis=0, keepdims=True))
    scaled = a * scale_rows * scale_cols
    ah[...], al[...] = split(scaled)
    w[...] = jnp.where(r_id == c_id, 1.5 - 0.5 * scaled, jnp.where(r_id > c_id, -scaled, 0.0))

    rb = lax.broadcasted_iota(jnp.int32, (B, B), 0)
    cb = lax.broadcasted_iota(jnp.int32, (B, B), 1)

    def correction(gram):
        return jnp.where(rb == cb, 0.5 - 0.5 * gram, jnp.where(rb > cb, -gram, 0.0)).astype(bf16)

    def apply(w0, w1, x00, x10, x11):
        p00, p10, p11 = correction(x00), (-x10).astype(bf16), correction(x11)
        w[:B, :B] += nn(p00, w0)
        w[B:, :B] += nn(p10, w0) + nn(p11, w1[:, :B])
        w[B:, B:] += nn(p11, w1[:, B:])

    def coarse(_, carry):
        w0, w1 = w[:B, :B].astype(bf16), w[B:, :].astype(bf16)
        y0 = nn(w0, ah[:B, :B]).astype(bf16)
        y1 = nn(w1, ah[...]).astype(bf16)
        apply(w0, w1, nt(y0, w0), nt(y1[:, :B], w0), nt(y1, w1))
        return carry

    def fine(_, carry):
        w0h, w0l = split(w[:B, :B])
        w1h, w1l = split(w[B:, :])
        y0h, y0l = split(nn3(w0h, w0l, ah[:B, :B], al[:B, :B]))
        y1h, y1l = split(nn3(w1h, w1l, ah[...], al[...]))
        apply(
            w0h, w1h, nt3(y0h, y0l, w0h, w0l), nt3(y1h[:, :B], y1l[:, :B], w0h, w0l), nt3(y1h, y1l, w1h, w1l)
        )
        return carry

    lax.fori_loop(0, COARSE, coarse, 0)

    @pl.when(jnp.logical_not(is_self))
    def _():
        for which in range(2):
            remote(which, 0).wait_recv()

    @pl.when(is_self)
    def _():
        for which in range(2):
            own(which).wait()

    launch(0)
    lax.fori_loop(0, FINE, fine, 0)
    arrive(0)
    launch(1)
    wh[...], wl[...] = split(w[...] * scale_cols)
    fetch.wait()

    def solve(tile, block):
        left_part = tile[:, :B] * mask_ref[block, 0].astype(f32)
        right_part = tile[:, B:] * mask_ref[block, 1].astype(f32)
        lh, ll = split(left_part)
        rh, rl = split(right_part)
        first = nt3(lh, ll, wh[:B, :B], wl[:B, :B])
        second = nt3(lh, ll, wh[B:, :B], wl[B:, :B]) + nt3(rh, rl, wh[B:, B:], wl[B:, B:])
        return first, second

    tiles = mine.shape[0] // B

    def rows_out(t):
        part = rows_at(t * B, B)
        return pltpu.make_async_copy(mine.at[part], rows_ref.at[part], rows_sem.at[t])

    def solve_mine(t, carry):
        part = rows_at(t * B, B)
        first, second = solve(mine[part, :], row * tiles + t)
        mine[part, :B] = first
        mine[part, B:] = second
        rows_out(t).start()
        return carry

    lax.fori_loop(0, 2, solve_mine, 0)
    arrive(1)
    launch(2)
    lax.fori_loop(2, tiles, solve_mine, 0)
    arrive(2)
    launch(3)
    arrive(3)

    needed = need.shape[0] // B

    def solve_need(t, carry):
        part = rows_at(t * B, B)
        first, second = solve(need[part, :], col * needed + t)
        ch_ref[part, :B], cl_ref[part, :B] = split(first)
        ch_ref[part, B:], cl_ref[part, B:] = split(second)
        return carry

    lax.fori_loop(0, needed, solve_need, 0)

    for step in range(4):
        for copy in sends(step):
            copy.wait_send()

    @pl.when(is_source)
    def _():
        for dx in range(1, 4):
            for which in range(2):
                remote(which, dx).wait_send()

    @pl.when(jnp.logical_and(is_source, jnp.logical_not(is_self)))
    def _():
        for which in range(2):
            remote(which, 0).wait_send()

    for t in range(tiles):
        rows_out(t).wait()


def update_kernel(rows_ref, ch_ref, cl_ref, slab_ref, rows_out, out_ref, max_ref):
    @pl.when(pl.program_id(0) == 0)
    def _():
        max_ref[...] = jnp.zeros_like(max_ref)

    rows = rows_ref[...]
    rows_out[...] = rows
    rh, rl = split(rows)
    step = 256
    for at in range(0, out_ref.shape[1], step):
        part = pl.ds(at, step)
        value = slab_ref[:, part] - nt3(rh, rl, ch_ref[part, :], cl_ref[part, :])
        out_ref[:, part] = value
        size = jnp.abs(value)
        size = jnp.max(size.reshape(-1, 8, step), axis=0)
        max_ref[...] = jnp.maximum(max_ref[...], jnp.maximum(size[:, :128], size[:, 128:]))


def growth_kernel(in_ref, out_ref, mid, cols_in, rows_in, col_send, col_recv, row_send, row_recv):
    row, col = lax.axis_index("row"), lax.axis_index("col")
    rows, cols = lax.axis_size("row"), lax.axis_size("col")
    barrier = pltpu.get_barrier_semaphore()
    for d in range(1, cols):
        pl.semaphore_signal(barrier, inc=1, device_id=(row, (col + d) % cols), device_id_type=MESH)
    for d in range(1, rows):
        pl.semaphore_signal(barrier, inc=1, device_id=((row + d) % rows, col), device_id_type=MESH)
    pl.semaphore_wait(barrier, rows + cols - 2)

    first = [
        pltpu.make_async_remote_copy(
            src_ref=in_ref, dst_ref=cols_in.at[d - 1], send_sem=col_send.at[d - 1], recv_sem=col_recv.at[d - 1],
            device_id=(row, (col + d) % cols), device_id_type=MESH,
        )
        for d in range(1, cols)
    ]
    for copy in first:
        copy.start()
    best = in_ref[...]
    for d in range(1, cols):
        first[d - 1].wait_recv()
        best = jnp.maximum(best, cols_in[d - 1])
    mid[...] = best
    second = [
        pltpu.make_async_remote_copy(
            src_ref=mid, dst_ref=rows_in.at[d - 1], send_sem=row_send.at[d - 1], recv_sem=row_recv.at[d - 1],
            device_id=((row + d) % rows, col), device_id_type=MESH,
        )
        for d in range(1, rows)
    ]
    for copy in second:
        copy.start()
    for d in range(1, rows):
        second[d - 1].wait_recv()
        best = jnp.maximum(best, rows_in[d - 1])
    out_ref[0, 0] = jnp.max(best)
    for copy in first + second:
        copy.wait_send()


def body(diag_block, panel, block_mask, slab):
    rows_dev, cols_dev = slab.shape
    tiles = rows_dev // B
    vmem = pl.BlockSpec(memory_space=pltpu.VMEM)
    smem = pl.BlockSpec(memory_space=pltpu.SMEM)
    hbm = pl.BlockSpec(memory_space=pl.ANY)
    dma = pltpu.SemaphoreType.DMA
    rows, ch, cl = pl.pallas_call(
        front_kernel,
        out_shape=(
            jax.ShapeDtypeStruct((rows_dev, PW), f32),
            jax.ShapeDtypeStruct((cols_dev, PW), bf16),
            jax.ShapeDtypeStruct((cols_dev, PW), bf16),
        ),
        in_specs=[vmem, smem, hbm],
        out_specs=(hbm, vmem, vmem),
        scratch_shapes=[
            pltpu.VMEM((PW, PW), bf16),
            pltpu.VMEM((PW, PW), bf16),
            pltpu.VMEM((PW, PW), f32),
            pltpu.VMEM((PW, PW), bf16),
            pltpu.VMEM((PW, PW), bf16),
            pltpu.VMEM((rows_dev, PW), f32),
            pltpu.VMEM((cols_dev, PW), f32),
            dma,
            dma((tiles,)),
            dma((2,)),
            dma((8,)),
            dma((2,)),
            dma((16,)),
            dma((16,)),
        ],
        compiler_params=pltpu.CompilerParams(
            collective_id=0, has_side_effects=True, vmem_limit_bytes=32 << 20
        ),
        name="front",
    )(diag_block, block_mask, panel)

    out_rows, updated, peak = pl.pallas_call(
        update_kernel,
        grid=(tiles,),
        out_shape=(
            jax.ShapeDtypeStruct((rows_dev, PW), f32),
            jax.ShapeDtypeStruct((rows_dev, cols_dev), f32),
            jax.ShapeDtypeStruct((8, 128), f32),
        ),
        in_specs=[
            pl.BlockSpec((B, PW), lambda i: (i, 0)),
            pl.BlockSpec((cols_dev, PW), lambda i: (0, 0)),
            pl.BlockSpec((cols_dev, PW), lambda i: (0, 0)),
            pl.BlockSpec((B, cols_dev), lambda i: (i, 0)),
        ],
        out_specs=(
            pl.BlockSpec((B, PW), lambda i: (i, 0)),
            pl.BlockSpec((B, cols_dev), lambda i: (i, 0)),
            pl.BlockSpec((8, 128), lambda i: (0, 0)),
        ),
        compiler_params=pltpu.CompilerParams(vmem_limit_bytes=32 << 20),
        name="update",
    )(rows, ch, cl, slab)

    n_rows, n_cols = lax.axis_size("row"), lax.axis_size("col")
    growth = pl.pallas_call(
        growth_kernel,
        out_shape=jax.ShapeDtypeStruct((1, 1), f32),
        in_specs=[vmem],
        out_specs=smem,
        scratch_shapes=[
            pltpu.VMEM((8, 128), f32),
            pltpu.VMEM((n_cols - 1, 8, 128), f32),
            pltpu.VMEM((n_rows - 1, 8, 128), f32),
            dma((n_cols - 1,)),
            dma((n_cols - 1,)),
            dma((n_rows - 1,)),
            dma((n_rows - 1,)),
        ],
        compiler_params=pltpu.CompilerParams(collective_id=1, has_side_effects=True),
        name="growth",
    )(peak)
    return (out_rows, updated, growth.reshape(()))


def solution(mesh):
    in_specs = (P(), P("row", None), P(), P("row", "col"))
    out_specs = (P("row", None), P("row", "col"), P())
    return jax.shard_map(body, mesh=mesh, in_specs=in_specs, out_specs=out_specs, check_vma=False)
```

```python
import jax
import jax.numpy as jnp
from jax import lax
from jax.experimental import pallas as pl
from jax.experimental.pallas import tpu as pltpu
from jax.sharding import PartitionSpec as P

B = 256
PW = 512
COARSE = 7
FINE = 3
MESH = pl.DeviceIdType.MESH
f32 = jnp.float32
bf16 = jnp.bfloat16


def nn(a, b):
    return lax.dot_general(a, b, (((1,), (0,)), ((), ())), preferred_element_type=f32)


def nt(a, b):
    return lax.dot_general(a, b, (((1,), (1,)), ((), ())), preferred_element_type=f32)


def split(a):
    high = a.astype(bf16)
    return high, (a - high.astype(f32)).astype(bf16)


def nt3(ah, al, bh, bl):
    return nt(ah, bh) + (nt(ah, bl) + nt(al, bh))


def nn3(ah, al, bh, bl):
    return nn(ah, bh) + (nn(ah, bl) + nn(al, bh))


def rows_at(start, size):
    return pl.ds(pl.multiple_of(start, 16), size)


def front_kernel(
    diag_hbm, mask_hbm, panel_hbm, slab_hbm, mine, near, slab_out,
    diag, mask, ah, al, w, wh, wl, need,
    diag_sem, mask_sem, panel_sem, slab_sem, self_sem, out_sem, in_sem, line_send, line_recv, ring_send, ring_recv,
):
    row, col = lax.axis_index("row"), lax.axis_index("col")
    z, x = row // 4, row % 4
    y, core = col // 2, col % 2
    half = need.shape[0] // 2
    piece = half // 16
    wide = 4 * piece

    is_source = row < 4
    is_self = jnp.logical_and(row == 0, y == 0)
    source = (y, z * 2 + core)

    def along_x(step):
        return z * 4 + (x + step) % 4

    def along_z(step):
        return ((z + step) % 4) * 4 + x

    fetch_diag = pltpu.make_async_copy(diag_hbm, diag, diag_sem)
    fetch_mask = pltpu.make_async_copy(mask_hbm, mask, mask_sem)
    fetch_panel = pltpu.make_async_copy(panel_hbm, mine, panel_sem)
    fetch_slab = pltpu.make_async_copy(slab_hbm, slab_out, slab_sem)
    fetch_diag.start()
    fetch_mask.start()

    barrier = pltpu.get_barrier_semaphore()

    def greet(device):
        pl.semaphore_signal(barrier, inc=1, device_id=device, device_id_type=MESH)

    @pl.when(jnp.logical_not(is_self))
    def _():
        greet(source)

    @pl.when(is_source)
    def _():
        for dx in range(1, 4):
            greet((y * 4 + dx, row * 2 + core))

    @pl.when(jnp.logical_and(is_source, jnp.logical_not(is_self)))
    def _():
        greet((y * 4, row * 2 + core))

    for step in range(1, 4):
        greet((along_x(step), col))
        greet((along_z(step), col))

    others = 1 - is_self.astype(jnp.int32)
    pl.semaphore_wait(barrier, 6 + others + jnp.where(is_source, 3 + others, 0))

    def spot(which, dz, dx):
        if which == 0:
            return (dz * 4 + dx) * piece
        return half + (dx * 4 + dz) * piece

    def scatter(which, dx):
        start = spot(which, y, dx)
        return (
            panel_hbm.at[rows_at(core * 2 * half + start, piece)],
            need.at[rows_at(start, piece)],
            (y * 4 + dx, row * 2 + core),
        )

    def remote(which, dx):
        src, dst, device = scatter(which, dx)
        return pltpu.make_async_remote_copy(
            src_ref=src, dst_ref=dst, send_sem=out_sem.at[which * 4 + dx], recv_sem=in_sem.at[which],
            device_id=device, device_id_type=MESH,
        )

    def own(which):
        src, dst, _ = scatter(which, 0)
        return pltpu.make_async_copy(src, dst, self_sem.at[which])

    @pl.when(is_source)
    def _():
        for which in range(2):
            for dx in range(1, 4):
                remote(which, dx).start()

    @pl.when(jnp.logical_and(is_source, jnp.logical_not(is_self)))
    def _():
        for which in range(2):
            remote(which, 0).start()

    @pl.when(is_self)
    def _():
        for which in range(2):
            own(which).start()

    fetch_panel.start()

    def hop(sems, index, start, size, device):
        part = need.at[rows_at(start, size)]
        return pltpu.make_async_remote_copy(
            src_ref=part, dst_ref=part, send_sem=sems[0].at[index], recv_sem=sems[1].at[index],
            device_id=(device, col), device_id_type=MESH,
        )

    line, ring = (line_send, line_recv), (ring_send, ring_recv)

    def line_hops(which):
        along = (along_x, along_z)[which]
        return [
            hop(line, 3 * which + step - 1, spot(which, z, x), piece, along(step)) for step in (2, 1, 3)
        ]

    def ring_hop(which, sign, stage):
        at, along = ((z, along_z), (x, along_x))[which]
        owner = at if stage < 2 else (at + 4 - sign) % 4
        part = stage % 2 if sign == 1 else 1 - stage % 2
        index = which * 6 + (0 if sign == 1 else 3) + stage
        return hop(ring, index, half * which + owner * wide + part * (wide // 2), wide // 2, along(sign % 4))

    fetch_diag.wait()
    a = diag[...]
    r_id = lax.broadcasted_iota(jnp.int32, (PW, PW), 0)
    c_id = lax.broadcasted_iota(jnp.int32, (PW, PW), 1)
    on_diag = jnp.where(r_id == c_id, a, 0.0)
    scale_rows = lax.rsqrt(jnp.sum(on_diag, axis=1, keepdims=True))
    scale_cols = lax.rsqrt(jnp.sum(on_diag, axis=0, keepdims=True))
    scaled = a * scale_rows * scale_cols
    ah[...], al[...] = split(scaled)
    w[...] = jnp.where(r_id == c_id, 1.5 - 0.5 * scaled, jnp.where(r_id > c_id, -scaled, 0.0))

    rb = lax.broadcasted_iota(jnp.int32, (B, B), 0)
    cb = lax.broadcasted_iota(jnp.int32, (B, B), 1)

    def correction(gram):
        return jnp.where(rb == cb, 0.5 - 0.5 * gram, jnp.where(rb > cb, -gram, 0.0)).astype(bf16)

    def apply(w0, w1, x00, x10, x11):
        p00, p10, p11 = correction(x00), (-x10).astype(bf16), correction(x11)
        w[:B, :B] += nn(p00, w0)
        w[B:, :B] += nn(p10, w0) + nn(p11, w1[:, :B])
        w[B:, B:] += nn(p11, w1[:, B:])

    def coarse(_, carry):
        w0, w1 = w[:B, :B].astype(bf16), w[B:, :].astype(bf16)
        y0 = nn(w0, ah[:B, :B]).astype(bf16)
        y1 = nn(w1, ah[...]).astype(bf16)
        apply(w0, w1, nt(y0, w0), nt(y1[:, :B], w0), nt(y1, w1))
        return carry

    def fine(_, carry):
        w0h, w0l = split(w[:B, :B])
        w1h, w1l = split(w[B:, :])
        y0h, y0l = split(nn3(w0h, w0l, ah[:B, :B], al[:B, :B]))
        y1h, y1l = split(nn3(w1h, w1l, ah[...], al[...]))
        apply(
            w0h, w1h, nt3(y0h, y0l, w0h, w0l), nt3(y1h[:, :B], y1l[:, :B], w0h, w0l), nt3(y1h, y1l, w1h, w1l)
        )
        return carry

    lax.fori_loop(0, COARSE, coarse, 0)

    @pl.when(jnp.logical_not(is_self))
    def _():
        for which in range(2):
            remote(which, 0).wait_recv()

    @pl.when(is_self)
    def _():
        for which in range(2):
            own(which).wait()

    for which in range(2):
        for copy in line_hops(which):
            copy.start()
    fetch_slab.start()
    lax.fori_loop(0, FINE, fine, 0)
    for which in range(2):
        for copy in line_hops(which):
            copy.wait_recv()
    for stage in range(2):
        for which in range(2):
            for sign in (1, -1):
                ring_hop(which, sign, stage).start()

    wh[...], wl[...] = split(w[...] * scale_cols)
    fetch_panel.wait()
    fetch_mask.wait()

    def solve(tile, block):
        left_part = tile[:, :B] * mask[0, block].astype(f32)
        right_part = tile[:, B:] * mask[1, block].astype(f32)
        lh, ll = split(left_part)
        rh, rl = split(right_part)
        first = nt3(lh, ll, wh[:B, :B], wl[:B, :B])
        second = nt3(lh, ll, wh[B:, :B], wl[B:, :B]) + nt3(rh, rl, wh[B:, B:], wl[B:, B:])
        return first, second

    tiles = mine.shape[0] // B

    def solve_mine(t, carry):
        part = rows_at(t * B, B)
        first, second = solve(mine[part, :], row * tiles + t)
        mine[part, :B] = first
        mine[part, B:] = second
        return carry

    def solve_need(start):
        part = rows_at(start, wide)
        first, second = solve(need[part, :], col * (2 * half // B) + start // B)
        for at, value in ((0, first), (B, second)):
            high, low = split(value)
            near[part, at:at + B] = high
            near[part, PW + at:PW + at + B] = low
            near[part, 2 * PW + at:2 * PW + at + B] = high

    lax.fori_loop(0, tiles, solve_mine, 0)
    for which in range(2):
        for sign in (1, -1):
            ring_hop(which, sign, 0).wait_recv()
            ring_hop(which, sign, 2).start()

    def quarter(which, step):
        return half * which + (((z, x)[which] + step) % 4) * wide

    for which in range(2):
        solve_need(quarter(which, 0))
    for which in range(2):
        for sign in (1, -1):
            ring_hop(which, sign, 1).wait_recv()
    for which in range(2):
        for step in (1, 3):
            solve_need(quarter(which, step))
    for which in range(2):
        for sign in (1, -1):
            ring_hop(which, sign, 2).wait_recv()
    for which in range(2):
        solve_need(quarter(which, 2))

    for which in range(2):
        for copy in line_hops(which):
            copy.wait_send()
        for sign in (1, -1):
            for stage in range(3):
                ring_hop(which, sign, stage).wait_send()

    @pl.when(is_source)
    def _():
        for dx in range(1, 4):
            for which in range(2):
                remote(which, dx).wait_send()

    @pl.when(jnp.logical_and(is_source, jnp.logical_not(is_self)))
    def _():
        for which in range(2):
            remote(which, 0).wait_send()

    fetch_slab.wait()


def update_kernel(rows_ref, near_ref, slab_ref, rows_out, out_ref, max_ref, rows_sem):
    tile = pl.program_id(0)

    @pl.when(tile == 0)
    def _():
        max_ref[...] = jnp.zeros_like(max_ref)
        pltpu.make_async_copy(rows_ref, rows_out, rows_sem).start()

    height = out_ref.shape[0]
    part = rows_at(tile * height, height)
    rh, rl = split(rows_ref[part, :])
    rows = jnp.concatenate([rh, rh, rl], axis=1)
    step = 256
    for at in range(0, out_ref.shape[1], step):
        value = slab_ref[part, at:at + step] - nt(rows, near_ref[at:at + step, :])
        out_ref[:, at:at + step] = value
        size = jnp.max(jnp.abs(value).reshape(-1, 8, step), axis=0)
        max_ref[...] = jnp.maximum(max_ref[...], jnp.maximum(size[:, :128], size[:, 128:]))

    @pl.when(tile == pl.num_programs(0) - 1)
    def _():
        pltpu.make_async_copy(rows_ref, rows_out, rows_sem).wait()


def far_first(size):
    return sorted(range(1, size), key=lambda d: -min(d, size - d))


def growth_kernel(in_ref, out_ref, mid, cols_in, rows_in, col_send, col_recv, row_send, row_recv):
    row, col = lax.axis_index("row"), lax.axis_index("col")
    rows, cols = lax.axis_size("row"), lax.axis_size("col")
    barrier = pltpu.get_barrier_semaphore()
    for d in range(1, cols):
        pl.semaphore_signal(barrier, inc=1, device_id=(row, (col + d) % cols), device_id_type=MESH)
    for d in range(1, rows):
        pl.semaphore_signal(barrier, inc=1, device_id=((row + d) % rows, col), device_id_type=MESH)
    pl.semaphore_wait(barrier, rows + cols - 2)

    first = {
        d: pltpu.make_async_remote_copy(
            src_ref=in_ref, dst_ref=cols_in.at[d - 1], send_sem=col_send.at[d - 1], recv_sem=col_recv.at[d - 1],
            device_id=(row, (col + d) % cols), device_id_type=MESH,
        )
        for d in far_first(cols)
    }
    for copy in first.values():
        copy.start()
    best = in_ref[...]
    for d in range(1, cols):
        first[d].wait_recv()
        best = jnp.maximum(best, cols_in[d - 1])
    mid[...] = best
    second = {
        d: pltpu.make_async_remote_copy(
            src_ref=mid, dst_ref=rows_in.at[d - 1], send_sem=row_send.at[d - 1], recv_sem=row_recv.at[d - 1],
            device_id=((row + d) % rows, col), device_id_type=MESH,
        )
        for d in far_first(rows)
    }
    for copy in second.values():
        copy.start()
    for d in range(1, rows):
        second[d].wait_recv()
        best = jnp.maximum(best, rows_in[d - 1])
    out_ref[0, 0] = jnp.max(best)
    for copy in [*first.values(), *second.values()]:
        copy.wait_send()


def body(diag_block, panel, block_mask, slab):
    rows_dev, cols_dev = slab.shape
    tiles = rows_dev // B
    vmem = pl.BlockSpec(memory_space=pltpu.VMEM)
    smem = pl.BlockSpec(memory_space=pltpu.SMEM)
    hbm = pl.BlockSpec(memory_space=pltpu.HBM)
    dma = pltpu.SemaphoreType.DMA
    marks = block_mask.T
    rows, near, slab_near = pl.pallas_call(
        front_kernel,
        out_shape=(
            jax.ShapeDtypeStruct((rows_dev, PW), f32),
            jax.ShapeDtypeStruct((cols_dev, 3 * PW), bf16),
            jax.ShapeDtypeStruct((rows_dev, cols_dev), f32),
        ),
        in_specs=[hbm, hbm, hbm, hbm],
        out_specs=(vmem, vmem, vmem),
        scratch_shapes=[
            pltpu.VMEM((PW, PW), f32),
            pltpu.SMEM(marks.shape, jnp.int32),
            pltpu.VMEM((PW, PW), bf16),
            pltpu.VMEM((PW, PW), bf16),
            pltpu.VMEM((PW, PW), f32),
            pltpu.VMEM((PW, PW), bf16),
            pltpu.VMEM((PW, PW), bf16),
            pltpu.VMEM((cols_dev, PW), f32),
            dma,
            dma,
            dma,
            dma,
            dma((2,)),
            dma((8,)),
            dma((2,)),
            dma((6,)),
            dma((6,)),
            dma((12,)),
            dma((12,)),
        ],
        compiler_params=pltpu.CompilerParams(
            collective_id=0, has_side_effects=True, vmem_limit_bytes=28 << 20
        ),
        name="front",
    )(*(pltpu.with_memory_space_constraint(a, pltpu.HBM) for a in (diag_block, marks, panel, slab)))

    out_rows, updated, peak = pl.pallas_call(
        update_kernel,
        grid=(tiles,),
        out_shape=(
            jax.ShapeDtypeStruct((rows_dev, PW), f32),
            jax.ShapeDtypeStruct((rows_dev, cols_dev), f32),
            jax.ShapeDtypeStruct((8, 128), f32),
        ),
        in_specs=[vmem, vmem, vmem],
        out_specs=(
            hbm,
            pl.BlockSpec((B, cols_dev), lambda i: (i, 0)),
            pl.BlockSpec((8, 128), lambda i: (0, 0)),
        ),
        scratch_shapes=[dma],
        compiler_params=pltpu.CompilerParams(vmem_limit_bytes=12 << 20),
        name="update",
    )(rows, near, slab_near)

    n_rows, n_cols = lax.axis_size("row"), lax.axis_size("col")
    growth = pl.pallas_call(
        growth_kernel,
        out_shape=jax.ShapeDtypeStruct((1, 1), f32),
        in_specs=[vmem],
        out_specs=smem,
        scratch_shapes=[
            pltpu.VMEM((8, 128), f32),
            pltpu.VMEM((n_cols - 1, 8, 128), f32),
            pltpu.VMEM((n_rows - 1, 8, 128), f32),
            dma((n_cols - 1,)),
            dma((n_cols - 1,)),
            dma((n_rows - 1,)),
            dma((n_rows - 1,)),
        ],
        compiler_params=pltpu.CompilerParams(collective_id=1, has_side_effects=True, vmem_limit_bytes=1 << 20),
        name="growth",
    )(peak)
    return (out_rows, updated, growth.reshape(()))


def solution(mesh):
    in_specs = (P(), P("row", None), P(), P("row", "col"))
    out_specs = (P("row", None), P("row", "col"), P())
    return jax.shard_map(body, mesh=mesh, in_specs=in_specs, out_specs=out_specs, check_vma=False)
```

```python
import jax
import jax.numpy as jnp
from jax import lax
from jax.experimental import pallas as pl
from jax.experimental.pallas import tpu as pltpu
from jax.sharding import PartitionSpec as P

B = 256
PW = 512
COARSE = 7
FINE = 2
EARLY = 3
TALL = 512
MESH = pl.DeviceIdType.MESH
f32 = jnp.float32
bf16 = jnp.bfloat16


def nn(a, b):
    return lax.dot_general(a, b, (((1,), (0,)), ((), ())), preferred_element_type=f32)


def nt(a, b):
    return lax.dot_general(a, b, (((1,), (1,)), ((), ())), preferred_element_type=f32)


def split(a):
    high = a.astype(bf16)
    return high, (a - high.astype(f32)).astype(bf16)


def nt3(ah, al, bh, bl):
    return nt(ah, bh) + (nt(ah, bl) + nt(al, bh))


def nn3(ah, al, bh, bl):
    return nn(ah, bh) + (nn(ah, bl) + nn(al, bh))


def rows_at(start, size):
    return pl.ds(pl.multiple_of(start, 16), size)


def far_first(size):
    return sorted(range(1, size), key=lambda d: -min(d, size - d))


def front_kernel(
    diag_hbm, mask_hbm, panel_hbm, slab_hbm, mine, slab, growth_ref,
    diag, mask, ah, al, w, wh, wl, rh, rl, gh, gl, need, peak, cols_in, rows_in,
    diag_sem, mask_sem, panel_sem, slab_sem, self_sem, out_sem, in_sem, line_send, line_recv, ring_send, ring_recv,
    col_send, col_recv, row_send, row_recv,
):
    row, col = lax.axis_index("row"), lax.axis_index("col")
    z, x = row // 4, row % 4
    y, core = col // 2, col % 2
    half = need.shape[0] // 2
    piece = half // 16
    wide = 4 * piece
    rows, cols = lax.axis_size("row"), lax.axis_size("col")

    is_source = row < 4
    is_self = jnp.logical_and(row == 0, y == 0)
    source = (y, z * 2 + core)

    def along_x(step):
        return z * 4 + (x + step) % 4

    def along_z(step):
        return ((z + step) % 4) * 4 + x

    fetch_diag = pltpu.make_async_copy(diag_hbm, diag, diag_sem)
    fetch_mask = pltpu.make_async_copy(mask_hbm, mask, mask_sem)
    fetch_panel = pltpu.make_async_copy(panel_hbm, mine, panel_sem)
    fetch_slab = pltpu.make_async_copy(slab_hbm, slab, slab_sem)
    fetch_diag.start()
    fetch_mask.start()

    barrier = pltpu.get_barrier_semaphore()

    def greet(device):
        pl.semaphore_signal(barrier, inc=1, device_id=device, device_id_type=MESH)

    @pl.when(jnp.logical_not(is_self))
    def _():
        greet(source)

    @pl.when(is_source)
    def _():
        for dx in range(1, 4):
            greet((y * 4 + dx, row * 2 + core))

    @pl.when(jnp.logical_and(is_source, jnp.logical_not(is_self)))
    def _():
        greet((y * 4, row * 2 + core))

    for step in range(1, 4):
        greet((along_x(step), col))
        greet((along_z(step), col))
    for d in range(1, cols):
        greet((row, (col + d) % cols))

    others = 1 - is_self.astype(jnp.int32)
    pl.semaphore_wait(barrier, 5 + cols + others + jnp.where(is_source, 3 + others, 0))

    def spot(which, dz, dx):
        if which == 0:
            return (dz * 4 + dx) * piece
        return half + (dx * 4 + dz) * piece

    def scatter(which, dx):
        start = spot(which, y, dx)
        return (
            panel_hbm.at[rows_at(core * 2 * half + start, piece)],
            need.at[rows_at(start, piece)],
            (y * 4 + dx, row * 2 + core),
        )

    def remote(which, dx):
        src, dst, device = scatter(which, dx)
        return pltpu.make_async_remote_copy(
            src_ref=src, dst_ref=dst, send_sem=out_sem.at[which * 4 + dx], recv_sem=in_sem.at[which],
            device_id=device, device_id_type=MESH,
        )

    def own(which):
        src, dst, _ = scatter(which, 0)
        return pltpu.make_async_copy(src, dst, self_sem.at[which])

    @pl.when(is_source)
    def _():
        for which in range(2):
            for dx in range(1, 4):
                remote(which, dx).start()

    @pl.when(jnp.logical_and(is_source, jnp.logical_not(is_self)))
    def _():
        for which in range(2):
            remote(which, 0).start()

    @pl.when(is_self)
    def _():
        for which in range(2):
            own(which).start()

    fetch_panel.start()

    def hop(sems, index, start, size, device):
        part = need.at[rows_at(start, size)]
        return pltpu.make_async_remote_copy(
            src_ref=part, dst_ref=part, send_sem=sems[0].at[index], recv_sem=sems[1].at[index],
            device_id=(device, col), device_id_type=MESH,
        )

    line, ring = (line_send, line_recv), (ring_send, ring_recv)

    def line_hops(which):
        along = (along_x, along_z)[which]
        return [
            hop(line, 3 * which + step - 1, spot(which, z, x), piece, along(step)) for step in (2, 1, 3)
        ]

    def ring_hop(which, sign, stage):
        at, along = ((z, along_z), (x, along_x))[which]
        owner = at if stage < 2 else (at + 4 - sign) % 4
        part = stage % 2 if sign == 1 else 1 - stage % 2
        index = which * 6 + (0 if sign == 1 else 3) + stage
        return hop(ring, index, half * which + owner * wide + part * (wide // 2), wide // 2, along(sign % 4))

    fetch_diag.wait()
    a = diag[...]
    r_id = lax.broadcasted_iota(jnp.int32, (PW, PW), 0)
    c_id = lax.broadcasted_iota(jnp.int32, (PW, PW), 1)
    on_diag = jnp.where(r_id == c_id, a, 0.0)
    scale_rows = lax.rsqrt(jnp.sum(on_diag, axis=1, keepdims=True))
    scale_cols = lax.rsqrt(jnp.sum(on_diag, axis=0, keepdims=True))
    scaled = a * scale_rows * scale_cols
    ah[...], al[...] = split(scaled)
    w[...] = jnp.where(r_id == c_id, 1.5 - 0.5 * scaled, jnp.where(r_id > c_id, -scaled, 0.0))

    rb = lax.broadcasted_iota(jnp.int32, (B, B), 0)
    cb = lax.broadcasted_iota(jnp.int32, (B, B), 1)

    def correction(gram):
        return jnp.where(rb == cb, 0.5 - 0.5 * gram, jnp.where(rb > cb, -gram, 0.0)).astype(bf16)

    def apply(w0, w1, x00, x10, x11):
        p00, p10, p11 = correction(x00), (-x10).astype(bf16), correction(x11)
        w[:B, :B] += nn(p00, w0)
        w[B:, :B] += nn(p10, w0) + nn(p11, w1[:, :B])
        w[B:, B:] += nn(p11, w1[:, B:])

    def coarse(_, carry):
        w0, w1 = w[:B, :B].astype(bf16), w[B:, :].astype(bf16)
        y0 = nn(w0, ah[:B, :B]).astype(bf16)
        y1 = nn(w1, ah[...]).astype(bf16)
        apply(w0, w1, nt(y0, w0), nt(y1[:, :B], w0), nt(y1, w1))
        return carry

    def fine(_, carry):
        w0h, w0l = split(w[:B, :B])
        w1h, w1l = split(w[B:, :])
        y0h, y0l = split(nn3(w0h, w0l, ah[:B, :B], al[:B, :B]))
        y1h, y1l = split(nn3(w1h, w1l, ah[...], al[...]))
        apply(
            w0h, w1h, nt3(y0h, y0l, w0h, w0l), nt3(y1h[:, :B], y1l[:, :B], w0h, w0l), nt3(y1h, y1l, w1h, w1l)
        )
        return carry

    lax.fori_loop(0, COARSE, coarse, 0)

    @pl.when(jnp.logical_not(is_self))
    def _():
        for which in range(2):
            remote(which, 0).wait_recv()

    @pl.when(is_self)
    def _():
        for which in range(2):
            own(which).wait()

    for which in range(2):
        for copy in line_hops(which):
            copy.start()
    fetch_slab.start()
    lax.fori_loop(0, FINE, fine, 0)
    wh[...], wl[...] = split(w[...] * scale_cols)
    fetch_panel.wait()
    fetch_mask.wait()

    def solve(left_part, right_part):
        lh, ll = split(left_part)
        qh, ql = split(right_part)
        first = nt3(lh, ll, wh[:B, :B], wl[:B, :B])
        second = nt3(lh, ll, wh[B:, :B], wl[B:, :B]) + nt3(qh, ql, wh[B:, B:], wl[B:, B:])
        return first, second

    tiles = mine.shape[0] // B

    def solve_mine(t, carry):
        part = rows_at(t * B, B)
        block = row * tiles + t
        parts = solve(mine[part, :B] * mask[0, block].astype(f32), mine[part, B:] * mask[1, block].astype(f32))
        for at, value in zip((0, B), parts):
            mine[part, at:at + B] = value
            rh[part, at:at + B], rl[part, at:at + B] = split(value)
        return carry

    lax.fori_loop(0, EARLY, solve_mine, 0)
    for which in range(2):
        for copy in line_hops(which):
            copy.wait_recv()
    for stage in range(2):
        for which in range(2):
            for sign in (1, -1):
                ring_hop(which, sign, stage).start()
    lax.fori_loop(EARLY, tiles, solve_mine, 0)
    for which in range(2):
        for sign in (1, -1):
            ring_hop(which, sign, 0).wait_recv()
            ring_hop(which, sign, 2).start()

    def masked_need(which, step):
        start = half * which + (((z, x)[which] + step) % 4) * wide
        part = rows_at(start, wide)
        block = col * (2 * half // B) + start // B
        left_part = need[part, :B] * mask[0, block].astype(f32)
        right_part = need[part, B:] * mask[1, block].astype(f32)
        return pl.ds(pl.multiple_of(start, 128), wide), left_part, right_part

    peak[...] = jnp.zeros_like(peak)

    def update(step):
        at0, left0, right0 = masked_need(0, step)
        at1, left1, right1 = masked_need(1, step)
        first, second = solve(jnp.concatenate([left0, left1], axis=0), jnp.concatenate([right0, right1], axis=0))
        gh[:, :B], gl[:, :B] = split(first)
        gh[:, B:], gl[:, B:] = split(second)

        def update_rows(t, carry):
            part = rows_at(t * TALL, TALL)
            product = nt3(rh[part, :], rl[part, :], gh[...], gl[...])
            for at, value in ((at0, product[:, :wide]), (at1, product[:, wide:])):
                value = slab[part, at] - value
                slab[part, at] = value
                size = jnp.max(jnp.abs(value).reshape(-1, 8, wide), axis=0)
                peak[0] = jnp.maximum(peak[0], size)
            return carry

        lax.fori_loop(0, mine.shape[0] // TALL, update_rows, 0)

    fetch_slab.wait()
    update(0)
    for which in range(2):
        for sign in (1, -1):
            ring_hop(which, sign, 1).wait_recv()
    update(1)
    update(3)
    for which in range(2):
        for sign in (1, -1):
            ring_hop(which, sign, 2).wait_recv()
    update(2)

    def share(src, dst, sems, d, device):
        return pltpu.make_async_remote_copy(
            src_ref=src, dst_ref=dst.at[d - 1], send_sem=sems[0].at[d - 1], recv_sem=sems[1].at[d - 1],
            device_id=device, device_id_type=MESH,
        )

    def share_cols(d):
        return share(peak.at[0], cols_in, (col_send, col_recv), d, (row, (col + d) % cols))

    def share_rows(d):
        return share(peak.at[1], rows_in, (row_send, row_recv), d, ((row + d) % rows, col))

    for d in far_first(cols):
        share_cols(d).start()
    best = peak[0]
    for d in range(1, cols):
        share_cols(d).wait_recv()
    for d in range(1, cols):
        best = jnp.maximum(best, cols_in[d - 1])
    peak[1] = best
    for d in far_first(rows):
        share_rows(d).start()

    for which in range(2):
        for copy in line_hops(which):
            copy.wait_send()
        for sign in (1, -1):
            for stage in range(3):
                ring_hop(which, sign, stage).wait_send()

    @pl.when(is_source)
    def _():
        for dx in range(1, 4):
            for which in range(2):
                remote(which, dx).wait_send()

    @pl.when(jnp.logical_and(is_source, jnp.logical_not(is_self)))
    def _():
        for which in range(2):
            remote(which, 0).wait_send()

    for d in range(1, cols):
        share_cols(d).wait_send()
    for d in range(1, rows):
        share_rows(d).wait_recv()
    for d in range(1, rows):
        best = jnp.maximum(best, rows_in[d - 1])
    growth_ref[0, 0] = jnp.max(best)
    for d in range(1, rows):
        share_rows(d).wait_send()


def store_kernel(rows_ref, slab_ref, rows_out, slab_out, sems):
    copies = []
    for src, dst in ((slab_ref, slab_out), (rows_ref, rows_out)):
        for at in range(0, src.shape[0], TALL):
            part = pl.ds(at, TALL)
            copies.append(pltpu.make_async_copy(src.at[part], dst.at[part], sems.at[len(copies)]))
    for copy in copies:
        copy.start()
    for copy in copies:
        copy.wait()


def body(diag_block, panel, block_mask, slab):
    rows_dev, cols_dev = slab.shape
    n_rows, n_cols = lax.axis_size("row"), lax.axis_size("col")
    vmem = pl.BlockSpec(memory_space=pltpu.VMEM)
    smem = pl.BlockSpec(memory_space=pltpu.SMEM)
    hbm = pl.BlockSpec(memory_space=pltpu.HBM)
    dma = pltpu.SemaphoreType.DMA
    marks = block_mask.T
    rows, updated, growth = pl.pallas_call(
        front_kernel,
        out_shape=(
            jax.ShapeDtypeStruct((rows_dev, PW), f32),
            jax.ShapeDtypeStruct((rows_dev, cols_dev), f32),
            jax.ShapeDtypeStruct((1, 1), f32),
        ),
        in_specs=[hbm, hbm, hbm, hbm],
        out_specs=(vmem, vmem, smem),
        scratch_shapes=[
            pltpu.VMEM((PW, PW), f32),
            pltpu.SMEM(marks.shape, jnp.int32),
            pltpu.VMEM((PW, PW), bf16),
            pltpu.VMEM((PW, PW), bf16),
            pltpu.VMEM((PW, PW), f32),
            pltpu.VMEM((PW, PW), bf16),
            pltpu.VMEM((PW, PW), bf16),
            pltpu.VMEM((rows_dev, PW), bf16),
            pltpu.VMEM((rows_dev, PW), bf16),
            pltpu.VMEM((B, PW), bf16),
            pltpu.VMEM((B, PW), bf16),
            pltpu.VMEM((cols_dev, PW), f32),
            pltpu.VMEM((2, 8, 128), f32),
            pltpu.VMEM((n_cols - 1, 8, 128), f32),
            pltpu.VMEM((n_rows - 1, 8, 128), f32),
            dma,
            dma,
            dma,
            dma,
            dma((2,)),
            dma((8,)),
            dma((2,)),
            dma((6,)),
            dma((6,)),
            dma((12,)),
            dma((12,)),
            dma((n_cols - 1,)),
            dma((n_cols - 1,)),
            dma((n_rows - 1,)),
            dma((n_rows - 1,)),
        ],
        compiler_params=pltpu.CompilerParams(
            collective_id=0, has_side_effects=True, vmem_limit_bytes=32 << 20
        ),
        name="front",
    )(*(pltpu.with_memory_space_constraint(a, pltpu.HBM) for a in (diag_block, marks, panel, slab)))

    out_rows, out_slab = pl.pallas_call(
        store_kernel,
        out_shape=(
            jax.ShapeDtypeStruct((rows_dev, PW), f32),
            jax.ShapeDtypeStruct((rows_dev, cols_dev), f32),
        ),
        in_specs=[vmem, vmem],
        out_specs=(hbm, hbm),
        scratch_shapes=[dma((2 * rows_dev // TALL,))],
        compiler_params=pltpu.CompilerParams(vmem_limit_bytes=1 << 20),
        name="store",
    )(rows, updated)
    return (out_rows, out_slab, growth.reshape(()))


def solution(mesh):
    in_specs = (P(), P("row", None), P(), P("row", "col"))
    out_specs = (P("row", None), P("row", "col"), P())
    return jax.shard_map(body, mesh=mesh, in_specs=in_specs, out_specs=out_specs, check_vma=False)
```

```python
import jax
import jax.numpy as jnp
from jax import lax
from jax.experimental import pallas as pl
from jax.experimental.pallas import tpu as pltpu
from jax.sharding import PartitionSpec as P

B = 256
PW = 512
COARSE = 7
FINE = 2
EARLY = 0
TALL = 512
UNROLL = 4
PANE = 512
MESH = pl.DeviceIdType.MESH
f32 = jnp.float32
bf16 = jnp.bfloat16


def nn(a, b):
    return lax.dot_general(a, b, (((1,), (0,)), ((), ())), preferred_element_type=f32)


def nt(a, b):
    return lax.dot_general(a, b, (((1,), (1,)), ((), ())), preferred_element_type=f32)


def split(a):
    high = a.astype(bf16)
    return high, (a - high.astype(f32)).astype(bf16)


def nt3(ah, al, bh, bl):
    return nt(ah, bh) + (nt(ah, bl) + nt(al, bh))


def nn3(ah, al, bh, bl):
    return nn(ah, bh) + (nn(ah, bl) + nn(al, bh))


def rows_at(start, size):
    return pl.ds(pl.multiple_of(start, 16), size)


def far_first(size):
    return sorted(range(1, size), key=lambda d: -min(d, size - d))


def front_kernel(
    diag_hbm, mask_hbm, panel_hbm, slab_hbm, mine, slab, growth_ref,
    diag, mask, gram, ah, al, w, wh, wl, rh, rl, gh, gl, need, peak, cols_in, rows_in,
    diag_sem, mask_sem, panel_sem, slab_sem, out_sem, in_sem, line_send, line_recv, ring_send, ring_recv,
    col_send, col_recv, row_send, row_recv,
):
    row, col = lax.axis_index("row"), lax.axis_index("col")
    z, x = row // 4, row % 4
    y, core = col // 2, col % 2
    half = need.shape[0] // 2
    piece = half // 16
    wide = 4 * piece
    rows, cols = lax.axis_size("row"), lax.axis_size("col")

    is_source = row < 4
    source = (y, ((y + 2 + z) % 4) * 2 + core)
    target_z = (y - row + 18) % 4

    def along_x(step):
        return z * 4 + (x + step) % 4

    def along_z(step):
        return ((z + step) % 4) * 4 + x

    fetch_diag = pltpu.make_async_copy(diag_hbm, diag, diag_sem)
    fetch_mask = pltpu.make_async_copy(mask_hbm, mask, mask_sem)
    fetch_panel = pltpu.make_async_copy(panel_hbm, mine, panel_sem)
    fetch_slab = pltpu.make_async_copy(slab_hbm, slab, slab_sem)
    fetch_diag.start()
    fetch_mask.start()

    barrier = pltpu.get_barrier_semaphore()

    def greet(device):
        pl.semaphore_signal(barrier, inc=1, device_id=device, device_id_type=MESH)

    greet(source)

    @pl.when(is_source)
    def _():
        for step in range(4):
            greet((target_z * 4 + (row + step) % 4, row * 2 + core))

    for step in range(1, 4):
        greet((along_x(step), col))
        greet((along_z(step), col))
    for d in range(1, cols):
        greet((row, (col + d) % cols))

    pl.semaphore_wait(barrier, 6 + cols + jnp.where(is_source, 4, 0))

    def spot(which, dz, dx):
        if which == 0:
            return (dz * 4 + dx) * piece
        return half + (dx * 4 + dz) * piece

    def scatter(which, step):
        dx = (row + step) % 4
        start = spot(which, target_z, dx)
        return pltpu.make_async_remote_copy(
            src_ref=panel_hbm.at[rows_at(core * 2 * half + start, piece)], dst_ref=need.at[rows_at(start, piece)],
            send_sem=out_sem.at[which * 4 + step], recv_sem=in_sem.at[which],
            device_id=(target_z * 4 + dx, row * 2 + core), device_id_type=MESH,
        )

    @pl.when(is_source)
    def _():
        for which in range(2):
            for step in (2, 1, 3, 0):
                scatter(which, step).start()

    fetch_panel.start()

    def hop(sems, index, start, size, device):
        part = need.at[rows_at(start, size)]
        return pltpu.make_async_remote_copy(
            src_ref=part, dst_ref=part, send_sem=sems[0].at[index], recv_sem=sems[1].at[index],
            device_id=(device, col), device_id_type=MESH,
        )

    line, ring = (line_send, line_recv), (ring_send, ring_recv)

    def line_hops(which):
        along = (along_x, along_z)[which]
        return [
            hop(line, 3 * which + step - 1, spot(which, z, x), piece, along(step)) for step in (2, 1, 3)
        ]

    def ring_hop(which, sign, stage):
        at, along = ((z, along_z), (x, along_x))[which]
        owner = at if stage < 2 else (at + 4 - sign) % 4
        part = stage % 2 if sign == 1 else 1 - stage % 2
        index = which * 6 + (0 if sign == 1 else 3) + stage
        return hop(ring, index, half * which + owner * wide + part * (wide // 2), wide // 2, along(sign % 4))

    fetch_diag.wait()
    a = diag[...]
    r_id = lax.broadcasted_iota(jnp.int32, (PW, PW), 0)
    c_id = lax.broadcasted_iota(jnp.int32, (PW, PW), 1)
    on_diag = jnp.where(r_id == c_id, a, 0.0)
    scale_rows = lax.rsqrt(jnp.sum(on_diag, axis=1, keepdims=True))
    scale_cols = lax.rsqrt(jnp.sum(on_diag, axis=0, keepdims=True))
    scaled = a * scale_rows * scale_cols
    ah[...], al[...] = split(scaled)
    w[...] = jnp.where(r_id == c_id, 1.0, 0.0)
    gram[...] = scaled

    rb = lax.broadcasted_iota(jnp.int32, (B, B), 0)
    cb = lax.broadcasted_iota(jnp.int32, (B, B), 1)

    def correction(gram):
        return jnp.where(rb == cb, 0.5 - 0.5 * gram, jnp.where(rb > cb, -gram, 0.0)).astype(bf16)

    def apply(w0, w1, x00, x10, x11):
        p00, p10, p11 = correction(x00), (-x10).astype(bf16), correction(x11)
        w[:B, :B] += nn(p00, w0)
        w[B:, :B] += nn(p10, w0) + nn(p11, w1[:, :B])
        w[B:, B:] += nn(p11, w1[:, B:])

    def coarse(_, carry):
        g00, g10, g11 = gram[:B, :B], gram[B:, :B], gram[B:, B:]
        w0, w1 = w[:B, :B].astype(bf16), w[B:, :].astype(bf16)
        p00, p10, p11 = correction(g00), (-g10).astype(bf16), correction(g11)
        b00, b10, b11 = g00.astype(bf16), g10.astype(bf16), g11.astype(bf16)
        z00 = g00 + nn(p00, b00)
        z10 = g10 + (nn(p10, b00) + nn(p11, b10))
        z11 = g11 + (nt(p10, b10) + nn(p11, b11))
        c00, c10, c11 = z00.astype(bf16), z10.astype(bf16), z11.astype(bf16)
        gram[:B, :B] = z00 + nt(c00, p00)
        gram[B:, :B] = z10 + nt(c10, p00)
        gram[B:, B:] = z11 + (nt(c10, p10) + nt(c11, p11))
        w[:B, :B] += nn(p00, w0)
        w[B:, :B] += nn(p10, w0) + nn(p11, w1[:, :B])
        w[B:, B:] += nn(p11, w1[:, B:])
        return carry

    def fine(_, carry):
        w0h, w0l = split(w[:B, :B])
        w1h, w1l = split(w[B:, :])
        y0h, y0l = split(nn3(w0h, w0l, ah[:B, :B], al[:B, :B]))
        y1h, y1l = split(nn3(w1h, w1l, ah[...], al[...]))
        apply(
            w0h, w1h, nt3(y0h, y0l, w0h, w0l), nt3(y1h[:, :B], y1l[:, :B], w0h, w0l), nt3(y1h, y1l, w1h, w1l)
        )
        return carry

    lax.fori_loop(0, COARSE, coarse, 0)

    for which in range(2):
        scatter(which, 0).wait_recv()

    for which in range(2):
        for copy in line_hops(which):
            copy.start()
    fetch_slab.start()
    lax.fori_loop(0, FINE, fine, 0)
    wh[...], wl[...] = split(w[...] * scale_cols)
    fetch_panel.wait()
    fetch_mask.wait()

    def solve(left_part, right_part):
        lh, ll = split(left_part)
        qh, ql = split(right_part)
        first = nt3(lh, ll, wh[:B, :B], wl[:B, :B])
        second = nt3(lh, ll, wh[B:, :B], wl[B:, :B]) + nt3(qh, ql, wh[B:, B:], wl[B:, B:])
        return first, second

    def marked(ref, start, size, first_block):
        halves = []
        for k in range(2):
            parts = [
                ref[rows_at(start + at, B), k * B:(k + 1) * B] * mask[k, first_block + at // B].astype(f32)
                for at in range(0, size, B)
            ]
            halves.append(jnp.concatenate(parts, axis=0))
        return halves

    panes = mine.shape[0] // PANE

    def solve_mine(t, carry):
        part = rows_at(t * PANE, PANE)
        parts = solve(*marked(mine, t * PANE, PANE, (row * panes + t) * (PANE // B)))
        for at, value in zip((0, B), parts):
            mine[part, at:at + B] = value
            rh[part, at:at + B], rl[part, at:at + B] = split(value)
        return carry

    lax.fori_loop(0, EARLY, solve_mine, 0, unroll=True)
    for which in range(2):
        for copy in line_hops(which):
            copy.wait_recv()
    for stage in range(2):
        for which in range(2):
            for sign in (1, -1):
                ring_hop(which, sign, stage).start()
    lax.fori_loop(EARLY, panes, solve_mine, 0, unroll=True)
    for which in range(2):
        for sign in (1, -1):
            ring_hop(which, sign, 0).wait_recv()
            ring_hop(which, sign, 2).start()

    def masked_need(which, step):
        start = half * which + (((z, x)[which] + step) % 4) * wide
        part = rows_at(start, wide)
        block = col * (2 * half // B) + start // B
        left_part = need[part, :B] * mask[0, block].astype(f32)
        right_part = need[part, B:] * mask[1, block].astype(f32)
        return pl.ds(pl.multiple_of(start, 128), wide), left_part, right_part

    peak[...] = jnp.zeros_like(peak)

    def update(step):
        at0, left0, right0 = masked_need(0, step)
        at1, left1, right1 = masked_need(1, step)
        first, second = solve(jnp.concatenate([left0, left1], axis=0), jnp.concatenate([right0, right1], axis=0))
        gh[:, :B], gl[:, :B] = split(first)
        gh[:, B:], gl[:, B:] = split(second)

        def update_rows(t, carry):
            part = rows_at(t * TALL, TALL)
            product = nt3(rh[part, :], rl[part, :], gh[...], gl[...])
            for at, value in ((at0, product[:, :wide]), (at1, product[:, wide:])):
                value = slab[part, at] - value
                slab[part, at] = value
                size = jnp.max(jnp.abs(value).reshape(-1, 8, wide), axis=0)
                peak[0] = jnp.maximum(peak[0], size)
            return carry

        lax.fori_loop(0, mine.shape[0] // TALL, update_rows, 0, unroll=UNROLL)

    fetch_slab.wait()
    update(0)
    for which in range(2):
        for sign in (1, -1):
            ring_hop(which, sign, 1).wait_recv()
    update(1)
    update(3)
    for which in range(2):
        for sign in (1, -1):
            ring_hop(which, sign, 2).wait_recv()
    update(2)

    def share(src, dst, sems, d, device):
        return pltpu.make_async_remote_copy(
            src_ref=src, dst_ref=dst.at[d - 1], send_sem=sems[0].at[d - 1], recv_sem=sems[1].at[d - 1],
            device_id=device, device_id_type=MESH,
        )

    def share_cols(d):
        return share(peak.at[0], cols_in, (col_send, col_recv), d, (row, (col + d) % cols))

    def share_rows(d):
        return share(peak.at[1], rows_in, (row_send, row_recv), d, ((row + d) % rows, col))

    for d in far_first(cols):
        share_cols(d).start()
    best = peak[0]
    for d in range(1, cols):
        share_cols(d).wait_recv()
    for d in range(1, cols):
        best = jnp.maximum(best, cols_in[d - 1])
    peak[1] = best
    for d in far_first(rows):
        share_rows(d).start()

    for which in range(2):
        for copy in line_hops(which):
            copy.wait_send()
        for sign in (1, -1):
            for stage in range(3):
                ring_hop(which, sign, stage).wait_send()

    @pl.when(is_source)
    def _():
        for which in range(2):
            for step in range(4):
                scatter(which, step).wait_send()

    for d in range(1, cols):
        share_cols(d).wait_send()
    for d in range(1, rows):
        share_rows(d).wait_recv()
    for d in range(1, rows):
        best = jnp.maximum(best, rows_in[d - 1])
    growth_ref[0, 0] = jnp.max(best)
    for d in range(1, rows):
        share_rows(d).wait_send()


def store_kernel(rows_ref, slab_ref, rows_out, slab_out, sems):
    copies = []
    for src, dst in ((slab_ref, slab_out), (rows_ref, rows_out)):
        for at in range(0, src.shape[0], TALL):
            part = pl.ds(at, TALL)
            copies.append(pltpu.make_async_copy(src.at[part], dst.at[part], sems.at[len(copies)]))
    for copy in copies:
        copy.start()
    for copy in copies:
        copy.wait()


def body(diag_block, panel, block_mask, slab):
    rows_dev, cols_dev = slab.shape
    n_rows, n_cols = lax.axis_size("row"), lax.axis_size("col")
    vmem = pl.BlockSpec(memory_space=pltpu.VMEM)
    smem = pl.BlockSpec(memory_space=pltpu.SMEM)
    hbm = pl.BlockSpec(memory_space=pltpu.HBM)
    dma = pltpu.SemaphoreType.DMA
    marks = block_mask.T
    rows, updated, growth = pl.pallas_call(
        front_kernel,
        out_shape=(
            jax.ShapeDtypeStruct((rows_dev, PW), f32),
            jax.ShapeDtypeStruct((rows_dev, cols_dev), f32),
            jax.ShapeDtypeStruct((1, 1), f32),
        ),
        in_specs=[hbm, hbm, hbm, hbm],
        out_specs=(vmem, vmem, smem),
        scratch_shapes=[
            pltpu.VMEM((PW, PW), f32),
            pltpu.SMEM(marks.shape, jnp.int32),
            pltpu.VMEM((PW, PW), f32),
            pltpu.VMEM((PW, PW), bf16),
            pltpu.VMEM((PW, PW), bf16),
            pltpu.VMEM((PW, PW), f32),
            pltpu.VMEM((PW, PW), bf16),
            pltpu.VMEM((PW, PW), bf16),
            pltpu.VMEM((rows_dev, PW), bf16),
            pltpu.VMEM((rows_dev, PW), bf16),
            pltpu.VMEM((B, PW), bf16),
            pltpu.VMEM((B, PW), bf16),
            pltpu.VMEM((cols_dev, PW), f32),
            pltpu.VMEM((2, 8, 128), f32),
            pltpu.VMEM((n_cols - 1, 8, 128), f32),
            pltpu.VMEM((n_rows - 1, 8, 128), f32),
            dma,
            dma,
            dma,
            dma,
            dma((8,)),
            dma((2,)),
            dma((6,)),
            dma((6,)),
            dma((12,)),
            dma((12,)),
            dma((n_cols - 1,)),
            dma((n_cols - 1,)),
            dma((n_rows - 1,)),
            dma((n_rows - 1,)),
        ],
        compiler_params=pltpu.CompilerParams(
            collective_id=0, has_side_effects=True, vmem_limit_bytes=32 << 20
        ),
        name="front",
    )(*(pltpu.with_memory_space_constraint(a, pltpu.HBM) for a in (diag_block, marks, panel, slab)))

    out_rows, out_slab = pl.pallas_call(
        store_kernel,
        out_shape=(
            jax.ShapeDtypeStruct((rows_dev, PW), f32),
            jax.ShapeDtypeStruct((rows_dev, cols_dev), f32),
        ),
        in_specs=[vmem, vmem],
        out_specs=(hbm, hbm),
        scratch_shapes=[dma((2 * rows_dev // TALL,))],
        compiler_params=pltpu.CompilerParams(vmem_limit_bytes=1 << 20),
        name="store",
    )(rows, updated)
    return (out_rows, out_slab, growth.reshape(()))


def solution(mesh):
    in_specs = (P(), P("row", None), P(), P("row", "col"))
    out_specs = (P("row", None), P("row", "col"), P())
    return jax.shard_map(body, mesh=mesh, in_specs=in_specs, out_specs=out_specs, check_vma=False)
```

```python
import jax
import jax.numpy as jnp
from jax import lax
from jax.experimental import pallas as pl
from jax.experimental.pallas import tpu as pltpu
from jax.sharding import PartitionSpec as P

B = 256
PW = 512
COARSE = 7
FINE = 2
EARLY = 0
TALL = 512
UNROLL = 4
PANE = 512
PASSED = {1: (0, 1), -1: (3, 2)}
MESH = pl.DeviceIdType.MESH
f32 = jnp.float32
bf16 = jnp.bfloat16


def nn(a, b):
    return lax.dot_general(a, b, (((1,), (0,)), ((), ())), preferred_element_type=f32)


def nt(a, b):
    return lax.dot_general(a, b, (((1,), (1,)), ((), ())), preferred_element_type=f32)


def split(a):
    high = a.astype(bf16)
    return high, (a - high.astype(f32)).astype(bf16)


def nt3(ah, al, bh, bl):
    return nt(ah, bh) + (nt(ah, bl) + nt(al, bh))


def nn3(ah, al, bh, bl):
    return nn(ah, bh) + (nn(ah, bl) + nn(al, bh))


def rows_at(start, size):
    return pl.ds(pl.multiple_of(start, 16), size)


def far_first(size):
    return sorted(range(1, size), key=lambda d: -min(d, size - d))


def front_kernel(
    diag_hbm, mask_hbm, panel_hbm, slab_hbm, mine, slab, growth_ref,
    diag, mask, gram, ah, al, w, wh, wl, rh, rl, gh, gl, need, peak, told, cols_in, rows_in,
    diag_sem, mask_sem, panel_sem, slab_sem, out_sem, in_sem, line_send, line_recv, ring_send, ring_recv,
    col_send, col_recv, row_send, row_recv,
):
    row, col = lax.axis_index("row"), lax.axis_index("col")
    z, x = row // 4, row % 4
    y, core = col // 2, col % 2
    half = need.shape[0] // 2
    piece = half // 16
    wide = 4 * piece
    rows, cols = lax.axis_size("row"), lax.axis_size("col")

    is_source = row < 4
    source = (y, ((y + 2 + z) % 4) * 2 + core)
    target_z = (y - row + 18) % 4

    def along_x(step):
        return z * 4 + (x + step) % 4

    def along_z(step):
        return ((z + step) % 4) * 4 + x

    fetch_diag = pltpu.make_async_copy(diag_hbm, diag, diag_sem)
    fetch_mask = pltpu.make_async_copy(mask_hbm, mask, mask_sem)
    fetch_panel = pltpu.make_async_copy(panel_hbm, mine, panel_sem)
    fetch_slab = pltpu.make_async_copy(slab_hbm, slab, slab_sem)
    fetch_diag.start()
    fetch_mask.start()

    barrier = pltpu.get_barrier_semaphore()

    def greet(device):
        pl.semaphore_signal(barrier, inc=1, device_id=device, device_id_type=MESH)

    greet(source)

    @pl.when(is_source)
    def _():
        for step in range(4):
            greet((target_z * 4 + (row + step) % 4, row * 2 + core))

    for step in range(1, 4):
        greet((along_x(step), col))
        greet((along_z(step), col))
    for d in range(1, cols):
        greet((row, (col + d) % cols))

    pl.semaphore_wait(barrier, 6 + cols + jnp.where(is_source, 4, 0))

    def spot(which, dz, dx):
        if which == 0:
            return (dz * 4 + dx) * piece
        return half + (dx * 4 + dz) * piece

    def scatter(which, step):
        dx = (row + step) % 4
        start = spot(which, target_z, dx)
        return pltpu.make_async_remote_copy(
            src_ref=panel_hbm.at[rows_at(core * 2 * half + start, piece)], dst_ref=need.at[rows_at(start, piece)],
            send_sem=out_sem.at[which * 4 + step], recv_sem=in_sem.at[which],
            device_id=(target_z * 4 + dx, row * 2 + core), device_id_type=MESH,
        )

    @pl.when(is_source)
    def _():
        for which in range(2):
            for step in (2, 1, 3, 0):
                scatter(which, step).start()

    fetch_panel.start()

    def hop(sems, index, start, size, device):
        part = need.at[rows_at(start, size)]
        return pltpu.make_async_remote_copy(
            src_ref=part, dst_ref=part, send_sem=sems[0].at[index], recv_sem=sems[1].at[index],
            device_id=(device, col), device_id_type=MESH,
        )

    line, ring = (line_send, line_recv), (ring_send, ring_recv)

    def line_hops(which):
        along = (along_x, along_z)[which]
        return [
            hop(line, 3 * which + step - 1, spot(which, z, x), piece, along(step)) for step in (2, 1, 3)
        ]

    def ring_hop(which, sign, index):
        at, fine_at, along = ((z, x, along_z), (x, z, along_x))[which]
        owner, offset = (at, index) if index < 4 else ((at + 4 - sign) % 4, PASSED[sign][index - 4])
        start = half * which + owner * wide + ((fine_at + offset) % 4) * piece
        return hop(ring, which * 12 + (0 if sign == 1 else 6) + index, start, piece, along(sign % 4))

    def ring_hops(plus, minus):
        for k in range(max(len(plus), len(minus))):
            for which in range(2):
                for sign, indices in ((1, plus), (-1, minus)):
                    if k < len(indices):
                        yield ring_hop(which, sign, indices[k])

    fetch_diag.wait()
    a = diag[...]
    r_id = lax.broadcasted_iota(jnp.int32, (PW, PW), 0)
    c_id = lax.broadcasted_iota(jnp.int32, (PW, PW), 1)
    on_diag = jnp.where(r_id == c_id, a, 0.0)
    scale_rows = lax.rsqrt(jnp.sum(on_diag, axis=1, keepdims=True))
    scale_cols = lax.rsqrt(jnp.sum(on_diag, axis=0, keepdims=True))
    scaled = a * scale_rows * scale_cols
    ah[...], al[...] = split(scaled)
    w[...] = jnp.where(r_id == c_id, 1.0, 0.0)
    gram[...] = scaled

    rb = lax.broadcasted_iota(jnp.int32, (B, B), 0)
    cb = lax.broadcasted_iota(jnp.int32, (B, B), 1)

    def correction(gram):
        return jnp.where(rb == cb, 0.5 - 0.5 * gram, jnp.where(rb > cb, -gram, 0.0)).astype(bf16)

    def apply(w0, w1, x00, x10, x11):
        p00, p10, p11 = correction(x00), (-x10).astype(bf16), correction(x11)
        w[:B, :B] += nn(p00, w0)
        w[B:, :B] += nn(p10, w0) + nn(p11, w1[:, :B])
        w[B:, B:] += nn(p11, w1[:, B:])

    def coarse(_, carry):
        g00, g10, g11 = gram[:B, :B], gram[B:, :B], gram[B:, B:]
        w0, w1 = w[:B, :B].astype(bf16), w[B:, :].astype(bf16)
        p00, p10, p11 = correction(g00), (-g10).astype(bf16), correction(g11)
        b00, b10, b11 = g00.astype(bf16), g10.astype(bf16), g11.astype(bf16)
        z00 = g00 + nn(p00, b00)
        z10 = g10 + (nn(p10, b00) + nn(p11, b10))
        z11 = g11 + (nt(p10, b10) + nn(p11, b11))
        c00, c10, c11 = z00.astype(bf16), z10.astype(bf16), z11.astype(bf16)
        gram[:B, :B] = z00 + nt(c00, p00)
        gram[B:, :B] = z10 + nt(c10, p00)
        gram[B:, B:] = z11 + (nt(c10, p10) + nt(c11, p11))
        w[:B, :B] += nn(p00, w0)
        w[B:, :B] += nn(p10, w0) + nn(p11, w1[:, :B])
        w[B:, B:] += nn(p11, w1[:, B:])
        return carry

    def fine(_, carry):
        w0h, w0l = split(w[:B, :B])
        w1h, w1l = split(w[B:, :])
        y0h, y0l = split(nn3(w0h, w0l, ah[:B, :B], al[:B, :B]))
        y1h, y1l = split(nn3(w1h, w1l, ah[...], al[...]))
        apply(
            w0h, w1h, nt3(y0h, y0l, w0h, w0l), nt3(y1h[:, :B], y1l[:, :B], w0h, w0l), nt3(y1h, y1l, w1h, w1l)
        )
        return carry

    lax.fori_loop(0, COARSE, coarse, 0)

    for which in range(2):
        scatter(which, 0).wait_recv()

    for which in range(2):
        for copy in line_hops(which):
            copy.start()
    for copy in ring_hops((0,), (0,)):
        copy.start()
    fetch_slab.start()
    lax.fori_loop(0, FINE, fine, 0)
    wh[...], wl[...] = split(w[...] * scale_cols)
    fetch_panel.wait()
    fetch_mask.wait()

    def solve(left_part, right_part):
        lh, ll = split(left_part)
        qh, ql = split(right_part)
        first = nt3(lh, ll, wh[:B, :B], wl[:B, :B])
        second = nt3(lh, ll, wh[B:, :B], wl[B:, :B]) + nt3(qh, ql, wh[B:, B:], wl[B:, B:])
        return first, second

    def marked(ref, start, size, first_block):
        halves = []
        for k in range(2):
            parts = [
                ref[rows_at(start + at, B), k * B:(k + 1) * B] * mask[k, first_block + at // B].astype(f32)
                for at in range(0, size, B)
            ]
            halves.append(jnp.concatenate(parts, axis=0))
        return halves

    panes = mine.shape[0] // PANE

    def solve_mine(t, carry):
        part = rows_at(t * PANE, PANE)
        parts = solve(*marked(mine, t * PANE, PANE, (row * panes + t) * (PANE // B)))
        for at, value in zip((0, B), parts):
            mine[part, at:at + B] = value
            rh[part, at:at + B], rl[part, at:at + B] = split(value)
        return carry

    lax.fori_loop(0, EARLY, solve_mine, 0, unroll=True)
    for which in range(2):
        for copy in line_hops(which):
            copy.wait_recv()
    for copy in ring_hops((1, 2, 3), (3, 2, 1)):
        copy.start()
    for copy in ring_hops((0,), (0,)):
        copy.wait_recv()
    for copy in ring_hops((4,), ()):
        copy.start()
    lax.fori_loop(EARLY, panes, solve_mine, 0, unroll=True)

    def masked_need(which, step):
        start = half * which + (((z, x)[which] + step) % 4) * wide
        part = rows_at(start, wide)
        block = col * (2 * half // B) + start // B
        left_part = need[part, :B] * mask[0, block].astype(f32)
        right_part = need[part, B:] * mask[1, block].astype(f32)
        return pl.ds(pl.multiple_of(start, 128), wide), left_part, right_part

    peak[...] = jnp.zeros_like(peak)

    def update(step):
        at0, left0, right0 = masked_need(0, step)
        at1, left1, right1 = masked_need(1, step)
        first, second = solve(jnp.concatenate([left0, left1], axis=0), jnp.concatenate([right0, right1], axis=0))
        gh[:, :B], gl[:, :B] = split(first)
        gh[:, B:], gl[:, B:] = split(second)

        def update_rows(t, carry):
            part = rows_at(t * TALL, TALL)
            product = nt3(rh[part, :], rl[part, :], gh[...], gl[...])
            for at, value in ((at0, product[:, :wide]), (at1, product[:, wide:])):
                value = slab[part, at] - value
                slab[part, at] = value
                size = jnp.max(jnp.abs(value).reshape(-1, 8, wide), axis=0)
                peak[...] = jnp.maximum(peak[...], size)
            return carry

        lax.fori_loop(0, mine.shape[0] // TALL, update_rows, 0, unroll=UNROLL)

    fetch_slab.wait()
    update(0)
    for copy in ring_hops((1,), (3, 2)):
        copy.wait_recv()
    for copy in ring_hops((5,), (4, 5)):
        copy.start()
    for copy in ring_hops((2, 3), (1,)):
        copy.wait_recv()
    update(1)
    update(3)
    for copy in ring_hops((4, 5), (4, 5)):
        copy.wait_recv()
    update(2)

    def share(src, dst, sems, d, device):
        return pltpu.make_async_remote_copy(
            src_ref=src, dst_ref=dst.at[d - 1], send_sem=sems[0].at[d - 1], recv_sem=sems[1].at[d - 1],
            device_id=device, device_id_type=MESH,
        )

    def share_cols(d):
        return share(told.at[0], cols_in, (col_send, col_recv), d, (row, (col + d) % cols))

    def share_rows(d):
        return share(told.at[1], rows_in, (row_send, row_recv), d, ((row + d) % rows, col))

    best = jnp.max(peak[...], axis=0, keepdims=True)
    told[0] = best
    for d in far_first(cols):
        share_cols(d).start()
    for d in range(1, cols):
        share_cols(d).wait_recv()
    for d in range(1, cols):
        best = jnp.maximum(best, cols_in[d - 1])
    told[1] = best
    for d in far_first(rows):
        share_rows(d).start()

    for which in range(2):
        for copy in line_hops(which):
            copy.wait_send()
    for copy in ring_hops(range(6), range(6)):
        copy.wait_send()

    @pl.when(is_source)
    def _():
        for which in range(2):
            for step in range(4):
                scatter(which, step).wait_send()

    for d in range(1, cols):
        share_cols(d).wait_send()
    for d in range(1, rows):
        share_rows(d).wait_recv()
    for d in range(1, rows):
        best = jnp.maximum(best, rows_in[d - 1])
    growth_ref[0, 0] = jnp.max(best)
    for d in range(1, rows):
        share_rows(d).wait_send()


def store_kernel(rows_ref, slab_ref, rows_out, slab_out, sems):
    copies = []
    for src, dst in ((slab_ref, slab_out), (rows_ref, rows_out)):
        for at in range(0, src.shape[0], TALL):
            part = pl.ds(at, TALL)
            copies.append(pltpu.make_async_copy(src.at[part], dst.at[part], sems.at[len(copies)]))
    for copy in copies:
        copy.start()
    for copy in copies:
        copy.wait()


def body(diag_block, panel, block_mask, slab):
    rows_dev, cols_dev = slab.shape
    n_rows, n_cols = lax.axis_size("row"), lax.axis_size("col")
    vmem = pl.BlockSpec(memory_space=pltpu.VMEM)
    smem = pl.BlockSpec(memory_space=pltpu.SMEM)
    hbm = pl.BlockSpec(memory_space=pltpu.HBM)
    dma = pltpu.SemaphoreType.DMA
    marks = block_mask.T
    rows, updated, growth = pl.pallas_call(
        front_kernel,
        out_shape=(
            jax.ShapeDtypeStruct((rows_dev, PW), f32),
            jax.ShapeDtypeStruct((rows_dev, cols_dev), f32),
            jax.ShapeDtypeStruct((1, 1), f32),
        ),
        in_specs=[hbm, hbm, hbm, hbm],
        out_specs=(vmem, vmem, smem),
        scratch_shapes=[
            pltpu.VMEM((PW, PW), f32),
            pltpu.SMEM(marks.shape, jnp.int32),
            pltpu.VMEM((PW, PW), f32),
            pltpu.VMEM((PW, PW), bf16),
            pltpu.VMEM((PW, PW), bf16),
            pltpu.VMEM((PW, PW), f32),
            pltpu.VMEM((PW, PW), bf16),
            pltpu.VMEM((PW, PW), bf16),
            pltpu.VMEM((rows_dev, PW), bf16),
            pltpu.VMEM((rows_dev, PW), bf16),
            pltpu.VMEM((B, PW), bf16),
            pltpu.VMEM((B, PW), bf16),
            pltpu.VMEM((cols_dev, PW), f32),
            pltpu.VMEM((8, 128), f32),
            pltpu.VMEM((2, 1, 128), f32),
            pltpu.VMEM((n_cols - 1, 1, 128), f32),
            pltpu.VMEM((n_rows - 1, 1, 128), f32),
            dma,
            dma,
            dma,
            dma,
            dma((8,)),
            dma((2,)),
            dma((6,)),
            dma((6,)),
            dma((24,)),
            dma((24,)),
            dma((n_cols - 1,)),
            dma((n_cols - 1,)),
            dma((n_rows - 1,)),
            dma((n_rows - 1,)),
        ],
        compiler_params=pltpu.CompilerParams(
            collective_id=0, has_side_effects=True, vmem_limit_bytes=32 << 20
        ),
        name="front",
    )(*(pltpu.with_memory_space_constraint(a, pltpu.HBM) for a in (diag_block, marks, panel, slab)))

    out_rows, out_slab = pl.pallas_call(
        store_kernel,
        out_shape=(
            jax.ShapeDtypeStruct((rows_dev, PW), f32),
            jax.ShapeDtypeStruct((rows_dev, cols_dev), f32),
        ),
        in_specs=[vmem, vmem],
        out_specs=(hbm, hbm),
        scratch_shapes=[dma((2 * rows_dev // TALL,))],
        compiler_params=pltpu.CompilerParams(vmem_limit_bytes=1 << 20),
        name="store",
    )(rows, updated)
    return (out_rows, out_slab, growth.reshape(()))


def solution(mesh):
    in_specs = (P(), P("row", None), P(), P("row", "col"))
    out_specs = (P("row", None), P("row", "col"), P())
    return jax.shard_map(body, mesh=mesh, in_specs=in_specs, out_specs=out_specs, check_vma=False)
```

```python
import jax
import jax.numpy as jnp
from jax import lax
from jax.experimental import pallas as pl
from jax.experimental.pallas import tpu as pltpu
from jax.sharding import PartitionSpec as P

B = 256
PW = 512
COARSE = 7
FINE = 2
TALL = 512
CHUNK = 512
UNROLL = 4
PANE = 512
PASSED = {1: (0, 1), -1: (3, 2)}
MESH = pl.DeviceIdType.MESH
f32 = jnp.float32
bf16 = jnp.bfloat16


def nn(a, b):
    return lax.dot_general(a, b, (((1,), (0,)), ((), ())), preferred_element_type=f32)


def nt(a, b):
    return lax.dot_general(a, b, (((1,), (1,)), ((), ())), preferred_element_type=f32)


def split(a):
    high = a.astype(bf16)
    return high, (a - high.astype(f32)).astype(bf16)


def nt3(ah, al, bh, bl):
    return nt(ah, bh) + (nt(ah, bl) + nt(al, bh))


def nn3(ah, al, bh, bl):
    return nn(ah, bh) + (nn(ah, bl) + nn(al, bh))


def rows_at(start, size):
    return pl.ds(pl.multiple_of(start, 16), size)


def far_first(size):
    return sorted(range(1, size), key=lambda d: -min(d, size - d))


def front_kernel(
    diag_hbm, mask_hbm, panel_hbm, slab_hbm, mine, slab, growth_ref,
    diag, mask, gram, ah, al, w, wh, wl, rh, rl, gh, gl, need, peak, told, cols_in, rows_in,
    diag_sem, mask_sem, panel_sem, slab_sem, out_sem, in_sem, line_send, line_recv, ring_send, ring_recv,
    col_send, col_recv, row_send, row_recv,
):
    row, col = lax.axis_index("row"), lax.axis_index("col")
    z, x = row // 4, row % 4
    y, core = col // 2, col % 2
    half = need.shape[0] // 2
    piece = half // 16
    wide = 4 * piece
    rows, cols = lax.axis_size("row"), lax.axis_size("col")

    is_source = row < 4
    source = (y, ((y + 2 + z) % 4) * 2 + core)
    target_z = (y - row + 18) % 4

    def along_x(step):
        return z * 4 + (x + step) % 4

    def along_z(step):
        return ((z + step) % 4) * 4 + x

    fetch_diag = pltpu.make_async_copy(diag_hbm, diag, diag_sem)
    fetch_mask = pltpu.make_async_copy(mask_hbm, mask, mask_sem)
    fetch_panel = pltpu.make_async_copy(panel_hbm, mine, panel_sem)
    fetch_slab = pltpu.make_async_copy(slab_hbm, slab, slab_sem)
    fetch_diag.start()
    fetch_mask.start()

    barrier = pltpu.get_barrier_semaphore()

    def greet(device):
        pl.semaphore_signal(barrier, inc=1, device_id=device, device_id_type=MESH)

    greet(source)

    @pl.when(is_source)
    def _():
        for step in range(4):
            greet((target_z * 4 + (row + step) % 4, row * 2 + core))

    for step in range(1, 4):
        greet((along_x(step), col))
        greet((along_z(step), col))
    for d in range(1, cols):
        greet((row, (col + d) % cols))

    pl.semaphore_wait(barrier, 6 + cols + jnp.where(is_source, 4, 0))

    def spot(which, dz, dx):
        if which == 0:
            return (dz * 4 + dx) * piece
        return half + (dx * 4 + dz) * piece

    def scatter(which, step):
        dx = (row + step) % 4
        start = spot(which, target_z, dx)
        return pltpu.make_async_remote_copy(
            src_ref=panel_hbm.at[rows_at(core * 2 * half + start, piece)], dst_ref=need.at[rows_at(start, piece)],
            send_sem=out_sem.at[which * 4 + step], recv_sem=in_sem.at[which],
            device_id=(target_z * 4 + dx, row * 2 + core), device_id_type=MESH,
        )

    @pl.when(is_source)
    def _():
        for which in range(2):
            for step in (2, 1, 3, 0):
                scatter(which, step).start()

    fetch_panel.start()

    def hop(sems, index, start, size, device):
        part = need.at[rows_at(start, size)]
        return pltpu.make_async_remote_copy(
            src_ref=part, dst_ref=part, send_sem=sems[0].at[index], recv_sem=sems[1].at[index],
            device_id=(device, col), device_id_type=MESH,
        )

    line, ring = (line_send, line_recv), (ring_send, ring_recv)

    def line_hops(which):
        along = (along_x, along_z)[which]
        return {step: hop(line, 3 * which + step - 1, spot(which, z, x), piece, along(step)) for step in (2, 1, 3)}

    def ring_hop(which, sign, index):
        at, fine_at, along = ((z, x, along_z), (x, z, along_x))[which]
        owner, offset = (at, index) if index < 4 else ((at + 4 - sign) % 4, PASSED[sign][index - 4])
        start = half * which + owner * wide + ((fine_at + offset) % 4) * piece
        return hop(ring, which * 12 + (0 if sign == 1 else 6) + index, start, piece, along(sign % 4))

    def ring_hops(which, plus, minus):
        for k in range(max(len(plus), len(minus))):
            for sign, indices in ((1, plus), (-1, minus)):
                if k < len(indices):
                    yield ring_hop(which, sign, indices[k])

    fetch_diag.wait()
    a = diag[...]
    r_id = lax.broadcasted_iota(jnp.int32, (PW, PW), 0)
    c_id = lax.broadcasted_iota(jnp.int32, (PW, PW), 1)
    on_diag = jnp.where(r_id == c_id, a, 0.0)
    scale_rows = lax.rsqrt(jnp.sum(on_diag, axis=1, keepdims=True))
    scale_cols = lax.rsqrt(jnp.sum(on_diag, axis=0, keepdims=True))
    scaled = a * scale_rows * scale_cols
    ah[...], al[...] = split(scaled)
    w[...] = jnp.where(r_id == c_id, 1.0, 0.0)
    gram[...] = scaled

    rb = lax.broadcasted_iota(jnp.int32, (B, B), 0)
    cb = lax.broadcasted_iota(jnp.int32, (B, B), 1)

    def correction(gram):
        return jnp.where(rb == cb, 0.5 - 0.5 * gram, jnp.where(rb > cb, -gram, 0.0)).astype(bf16)

    def apply(w0, w1, x00, x10, x11):
        p00, p10, p11 = correction(x00), (-x10).astype(bf16), correction(x11)
        w[:B, :B] += nn(p00, w0)
        w[B:, :B] += nn(p10, w0) + nn(p11, w1[:, :B])
        w[B:, B:] += nn(p11, w1[:, B:])

    def coarse(_, carry):
        g00, g10, g11 = gram[:B, :B], gram[B:, :B], gram[B:, B:]
        w0, w1 = w[:B, :B].astype(bf16), w[B:, :].astype(bf16)
        p00, p10, p11 = correction(g00), (-g10).astype(bf16), correction(g11)
        b00, b10, b11 = g00.astype(bf16), g10.astype(bf16), g11.astype(bf16)
        z00 = g00 + nn(p00, b00)
        z10 = g10 + (nn(p10, b00) + nn(p11, b10))
        z11 = g11 + (nt(p10, b10) + nn(p11, b11))
        c00, c10, c11 = z00.astype(bf16), z10.astype(bf16), z11.astype(bf16)
        gram[:B, :B] = z00 + nt(c00, p00)
        gram[B:, :B] = z10 + nt(c10, p00)
        gram[B:, B:] = z11 + (nt(c10, p10) + nt(c11, p11))
        w[:B, :B] += nn(p00, w0)
        w[B:, :B] += nn(p10, w0) + nn(p11, w1[:, :B])
        w[B:, B:] += nn(p11, w1[:, B:])
        return carry

    def fine(_, carry):
        w0h, w0l = split(w[:B, :B])
        w1h, w1l = split(w[B:, :])
        y0h, y0l = split(nn3(w0h, w0l, ah[:B, :B], al[:B, :B]))
        y1h, y1l = split(nn3(w1h, w1l, ah[...], al[...]))
        apply(
            w0h, w1h, nt3(y0h, y0l, w0h, w0l), nt3(y1h[:, :B], y1l[:, :B], w0h, w0l), nt3(y1h, y1l, w1h, w1l)
        )
        return carry

    lax.fori_loop(0, COARSE, coarse, 0)
    lax.fori_loop(0, FINE, fine, 0)
    wh[...], wl[...] = split(w[...] * scale_cols)

    def begin(which):
        scatter(which, 0).wait_recv()
        for copy in line_hops(which).values():
            copy.start()
        for copy in ring_hops(which, (0,), (0,)):
            copy.start()

    def feed_near(which):
        for step in (1, 3):
            line_hops(which)[step].wait_recv()
        for copy in ring_hops(which, (1, 3), (3, 1)):
            copy.start()

    def feed_far(which):
        line_hops(which)[2].wait_recv()
        for copy in ring_hops(which, (2,), (2,)):
            copy.start()

    def pass_on(which):
        for copy in ring_hops(which, (0, 1), (0, 3, 2)):
            copy.wait_recv()
        for copy in ring_hops(which, (4, 5), (4, 5)):
            copy.start()
        for copy in ring_hops(which, (3, 2), (1,)):
            copy.wait_recv()

    begin(0)
    begin(1)
    fetch_slab.start()
    fetch_panel.wait()
    fetch_mask.wait()

    def solve(left_part, right_part):
        lh, ll = split(left_part)
        qh, ql = split(right_part)
        first = nt3(lh, ll, wh[:B, :B], wl[:B, :B])
        second = nt3(lh, ll, wh[B:, :B], wl[B:, :B]) + nt3(qh, ql, wh[B:, B:], wl[B:, B:])
        return first, second

    def marked(ref, start, size, first_block):
        halves = []
        for k in range(2):
            parts = [
                ref[rows_at(start + at, B), k * B:(k + 1) * B] * mask[k, first_block + at // B].astype(f32)
                for at in range(0, size, B)
            ]
            halves.append(jnp.concatenate(parts, axis=0))
        return halves

    panes = mine.shape[0] // PANE

    def solve_mine(t, carry):
        part = rows_at(t * PANE, PANE)
        parts = solve(*marked(mine, t * PANE, PANE, (row * panes + t) * (PANE // B)))
        for at, value in zip((0, B), parts):
            mine[part, at:at + B] = value
            rh[part, at:at + B], rl[part, at:at + B] = split(value)
        return carry

    lax.fori_loop(0, panes // 2, solve_mine, 0, unroll=True)
    feed_near(0)
    feed_far(0)
    lax.fori_loop(panes // 2, 3 * panes // 4, solve_mine, 0, unroll=True)
    feed_near(1)
    lax.fori_loop(3 * panes // 4, panes, solve_mine, 0, unroll=True)
    feed_far(1)

    def masked_need(which, step):
        start = half * which + (((z, x)[which] + step) % 4) * wide
        part = rows_at(start, wide)
        block = col * (2 * half // B) + start // B
        left_part = need[part, :B] * mask[0, block].astype(f32)
        right_part = need[part, B:] * mask[1, block].astype(f32)
        return pl.ds(pl.multiple_of(start, 128), wide), left_part, right_part

    peak[...] = jnp.zeros_like(peak)

    def update(one, two):
        at0, left0, right0 = masked_need(*one)
        at1, left1, right1 = masked_need(*two)
        first, second = solve(jnp.concatenate([left0, left1], axis=0), jnp.concatenate([right0, right1], axis=0))
        gh[:, :B], gl[:, :B] = split(first)
        gh[:, B:], gl[:, B:] = split(second)

        def update_rows(t, carry):
            part = rows_at(t * TALL, TALL)
            product = nt3(rh[part, :], rl[part, :], gh[...], gl[...])
            for at, value in ((at0, product[:, :wide]), (at1, product[:, wide:])):
                value = slab[part, at] - value
                slab[part, at] = value
                size = jnp.max(jnp.abs(value).reshape(-1, 8, wide), axis=0)
                peak[...] = jnp.maximum(peak[...], size)
            return carry

        lax.fori_loop(0, mine.shape[0] // TALL, update_rows, 0, unroll=UNROLL)

    fetch_slab.wait()
    update((0, 0), (1, 0))
    pass_on(0)
    update((0, 1), (0, 3))
    pass_on(1)
    update((1, 1), (1, 3))
    for which in range(2):
        for copy in ring_hops(which, (4, 5), (4, 5)):
            copy.wait_recv()
    update((0, 2), (1, 2))

    def share(src, dst, sems, d, device):
        return pltpu.make_async_remote_copy(
            src_ref=src, dst_ref=dst.at[d - 1], send_sem=sems[0].at[d - 1], recv_sem=sems[1].at[d - 1],
            device_id=device, device_id_type=MESH,
        )

    def share_cols(d):
        return share(told.at[0], cols_in, (col_send, col_recv), d, (row, (col + d) % cols))

    def share_rows(d):
        return share(told.at[1], rows_in, (row_send, row_recv), d, ((row + d) % rows, col))

    best = jnp.max(peak[...], axis=0, keepdims=True)
    told[0] = best
    for d in far_first(cols):
        share_cols(d).start()
    for d in range(1, cols):
        share_cols(d).wait_recv()
    for d in range(1, cols):
        best = jnp.maximum(best, cols_in[d - 1])
    told[1] = best
    for d in far_first(rows):
        share_rows(d).start()

    for which in range(2):
        for copy in line_hops(which).values():
            copy.wait_send()
        for copy in ring_hops(which, range(6), range(6)):
            copy.wait_send()

    @pl.when(is_source)
    def _():
        for which in range(2):
            for step in range(4):
                scatter(which, step).wait_send()

    for d in range(1, cols):
        share_cols(d).wait_send()
    for d in range(1, rows):
        share_rows(d).wait_recv()
    for d in range(1, rows):
        best = jnp.maximum(best, rows_in[d - 1])
    growth_ref[0, 0] = jnp.max(best)
    for d in range(1, rows):
        share_rows(d).wait_send()


def store_kernel(rows_ref, slab_ref, rows_out, slab_out, sems):
    copies = []
    for src, dst in ((slab_ref, slab_out), (rows_ref, rows_out)):
        for at in range(0, src.shape[0], CHUNK):
            part = pl.ds(at, CHUNK)
            copies.append(pltpu.make_async_copy(src.at[part], dst.at[part], sems.at[len(copies)]))
    for copy in copies:
        copy.start()
    for copy in copies:
        copy.wait()


def body(diag_block, panel, block_mask, slab):
    rows_dev, cols_dev = slab.shape
    n_rows, n_cols = lax.axis_size("row"), lax.axis_size("col")
    vmem = pl.BlockSpec(memory_space=pltpu.VMEM)
    smem = pl.BlockSpec(memory_space=pltpu.SMEM)
    hbm = pl.BlockSpec(memory_space=pltpu.HBM)
    dma = pltpu.SemaphoreType.DMA
    marks = block_mask.T
    rows, updated, growth = pl.pallas_call(
        front_kernel,
        out_shape=(
            jax.ShapeDtypeStruct((rows_dev, PW), f32),
            jax.ShapeDtypeStruct((rows_dev, cols_dev), f32),
            jax.ShapeDtypeStruct((1, 1), f32),
        ),
        in_specs=[hbm, hbm, hbm, hbm],
        out_specs=(vmem, vmem, smem),
        scratch_shapes=[
            pltpu.VMEM((PW, PW), f32),
            pltpu.SMEM(marks.shape, jnp.int32),
            pltpu.VMEM((PW, PW), f32),
            pltpu.VMEM((PW, PW), bf16),
            pltpu.VMEM((PW, PW), bf16),
            pltpu.VMEM((PW, PW), f32),
            pltpu.VMEM((PW, PW), bf16),
            pltpu.VMEM((PW, PW), bf16),
            pltpu.VMEM((rows_dev, PW), bf16),
            pltpu.VMEM((rows_dev, PW), bf16),
            pltpu.VMEM((B, PW), bf16),
            pltpu.VMEM((B, PW), bf16),
            pltpu.VMEM((cols_dev, PW), f32),
            pltpu.VMEM((8, 128), f32),
            pltpu.VMEM((2, 1, 128), f32),
            pltpu.VMEM((n_cols - 1, 1, 128), f32),
            pltpu.VMEM((n_rows - 1, 1, 128), f32),
            dma,
            dma,
            dma,
            dma,
            dma((8,)),
            dma((2,)),
            dma((6,)),
            dma((6,)),
            dma((24,)),
            dma((24,)),
            dma((n_cols - 1,)),
            dma((n_cols - 1,)),
            dma((n_rows - 1,)),
            dma((n_rows - 1,)),
        ],
        compiler_params=pltpu.CompilerParams(
            collective_id=0, has_side_effects=True, vmem_limit_bytes=32 << 20
        ),
        name="front",
    )(*(pltpu.with_memory_space_constraint(a, pltpu.HBM) for a in (diag_block, marks, panel, slab)))

    out_rows, out_slab = pl.pallas_call(
        store_kernel,
        out_shape=(
            jax.ShapeDtypeStruct((rows_dev, PW), f32),
            jax.ShapeDtypeStruct((rows_dev, cols_dev), f32),
        ),
        in_specs=[vmem, vmem],
        out_specs=(hbm, hbm),
        scratch_shapes=[dma((2 * rows_dev // CHUNK,))],
        compiler_params=pltpu.CompilerParams(vmem_limit_bytes=1 << 20),
        name="store",
    )(rows, updated)
    return (out_rows, out_slab, growth.reshape(()))


def solution(mesh):
    in_specs = (P(), P("row", None), P(), P("row", "col"))
    out_specs = (P("row", None), P("row", "col"), P())
    return jax.shard_map(body, mesh=mesh, in_specs=in_specs, out_specs=out_specs, check_vma=False)
```

```python
import jax
import jax.numpy as jnp
from jax import lax
from jax.experimental import pallas as pl
from jax.experimental.pallas import tpu as pltpu
from jax.sharding import PartitionSpec as P

B = 256
PW = 512
COARSE = 8
FINE = 2
TALL = 512
CHUNK = 512
UNROLL = 4
PANE = 512
PASSED = {1: (0, 1), -1: (3, 2)}
MESH = pl.DeviceIdType.MESH
f32 = jnp.float32
bf16 = jnp.bfloat16


def nn(a, b):
    return lax.dot_general(a, b, (((1,), (0,)), ((), ())), preferred_element_type=f32)


def nt(a, b):
    return lax.dot_general(a, b, (((1,), (1,)), ((), ())), preferred_element_type=f32)


def split(a):
    high = a.astype(bf16)
    return high, (a - high.astype(f32)).astype(bf16)


def nt3(ah, al, bh, bl):
    return nt(ah, bh) + (nt(ah, bl) + nt(al, bh))


def nn3(ah, al, bh, bl):
    return nn(ah, bh) + (nn(ah, bl) + nn(al, bh))


def rows_at(start, size):
    return pl.ds(pl.multiple_of(start, 16), size)


def far_first(size):
    return sorted(range(1, size), key=lambda d: -min(d, size - d))


def front_kernel(
    diag_hbm, mask_hbm, panel_hbm, slab_hbm, mine, slab, growth_ref,
    diag, mask, gram, ah, al, w, wh, wl, rh, rl, gh, gl, need, peak, told, cols_in, rows_in,
    diag_sem, mask_sem, panel_sem, slab_sem, out_sem, in_sem, line_send, line_recv, ring_send, ring_recv,
    col_send, col_recv, row_send, row_recv,
):
    row, col = lax.axis_index("row"), lax.axis_index("col")
    z, x = row // 4, row % 4
    y, core = col // 2, col % 2
    half = need.shape[0] // 2
    piece = half // 16
    wide = 4 * piece
    rows, cols = lax.axis_size("row"), lax.axis_size("col")

    is_source = row < 4
    source = (y, ((y + 2 + z) % 4) * 2 + core)
    target_z = (y - row + 18) % 4

    def along_x(step):
        return z * 4 + (x + step) % 4

    def along_z(step):
        return ((z + step) % 4) * 4 + x

    fetch_diag = pltpu.make_async_copy(diag_hbm, diag, diag_sem)
    fetch_mask = pltpu.make_async_copy(mask_hbm, mask, mask_sem)
    fetch_panel = pltpu.make_async_copy(panel_hbm, mine, panel_sem)
    fetch_slab = pltpu.make_async_copy(slab_hbm, slab, slab_sem)
    fetch_diag.start()
    fetch_mask.start()

    barrier = pltpu.get_barrier_semaphore()

    def greet(device):
        pl.semaphore_signal(barrier, inc=1, device_id=device, device_id_type=MESH)

    greet(source)

    @pl.when(is_source)
    def _():
        for step in range(4):
            greet((target_z * 4 + (row + step) % 4, row * 2 + core))

    for step in range(1, 4):
        greet((along_x(step), col))
        greet((along_z(step), col))
    for d in range(1, cols):
        greet((row, (col + d) % cols))

    pl.semaphore_wait(barrier, 6 + cols + jnp.where(is_source, 4, 0))

    def spot(which, dz, dx):
        if which == 0:
            return (dz * 4 + dx) * piece
        return half + (dx * 4 + dz) * piece

    def scatter(which, step):
        dx = (row + step) % 4
        start = spot(which, target_z, dx)
        return pltpu.make_async_remote_copy(
            src_ref=panel_hbm.at[rows_at(core * 2 * half + start, piece)], dst_ref=need.at[rows_at(start, piece)],
            send_sem=out_sem.at[which * 4 + step], recv_sem=in_sem.at[which],
            device_id=(target_z * 4 + dx, row * 2 + core), device_id_type=MESH,
        )

    @pl.when(is_source)
    def _():
        for which in range(2):
            for step in (2, 1, 3, 0):
                scatter(which, step).start()

    fetch_panel.start()

    def hop(sems, index, start, size, device):
        part = need.at[rows_at(start, size)]
        return pltpu.make_async_remote_copy(
            src_ref=part, dst_ref=part, send_sem=sems[0].at[index], recv_sem=sems[1].at[index],
            device_id=(device, col), device_id_type=MESH,
        )

    line, ring = (line_send, line_recv), (ring_send, ring_recv)

    def line_hops(which):
        along = (along_x, along_z)[which]
        return {step: hop(line, 3 * which + step - 1, spot(which, z, x), piece, along(step)) for step in (2, 1, 3)}

    def ring_hop(which, sign, index):
        at, fine_at, along = ((z, x, along_z), (x, z, along_x))[which]
        owner, offset = (at, index) if index < 4 else ((at + 4 - sign) % 4, PASSED[sign][index - 4])
        start = half * which + owner * wide + ((fine_at + offset) % 4) * piece
        return hop(ring, which * 12 + (0 if sign == 1 else 6) + index, start, piece, along(sign % 4))

    def ring_hops(which, plus, minus):
        for k in range(max(len(plus), len(minus))):
            for sign, indices in ((1, plus), (-1, minus)):
                if k < len(indices):
                    yield ring_hop(which, sign, indices[k])

    fetch_diag.wait()
    a = diag[...]
    r_id = lax.broadcasted_iota(jnp.int32, (PW, PW), 0)
    c_id = lax.broadcasted_iota(jnp.int32, (PW, PW), 1)
    on_diag = jnp.where(r_id == c_id, a, 0.0)
    scale_rows = lax.rsqrt(jnp.sum(on_diag, axis=1, keepdims=True))
    scale_cols = lax.rsqrt(jnp.sum(on_diag, axis=0, keepdims=True))
    scaled = a * scale_rows * scale_cols
    ah[...], al[...] = split(scaled)
    w[...] = jnp.where(r_id == c_id, 1.0, 0.0)
    gram[...] = scaled

    rb = lax.broadcasted_iota(jnp.int32, (B, B), 0)
    cb = lax.broadcasted_iota(jnp.int32, (B, B), 1)

    def correction(gram):
        return jnp.where(rb == cb, 0.5 - 0.5 * gram, jnp.where(rb > cb, -gram, 0.0)).astype(bf16)

    def apply(w0, w1, x00, x10, x11):
        p00, p10, p11 = correction(x00), (-x10).astype(bf16), correction(x11)
        w[:B, :B] += nn(p00, w0)
        w[B:, :B] += nn(p10, w0) + nn(p11, w1[:, :B])
        w[B:, B:] += nn(p11, w1[:, B:])

    def coarse(_, carry):
        g00, g10, g11 = gram[:B, :B], gram[B:, :B], gram[B:, B:]
        w0, w1 = w[:B, :B].astype(bf16), w[B:, :].astype(bf16)
        p00, p10, p11 = correction(g00), (-g10).astype(bf16), correction(g11)
        b00, b10, b11 = g00.astype(bf16), g10.astype(bf16), g11.astype(bf16)
        z00 = g00 + nn(p00, b00)
        z10 = g10 + (nn(p10, b00) + nn(p11, b10))
        z11 = g11 + (nt(p10, b10) + nn(p11, b11))
        c00, c10, c11 = z00.astype(bf16), z10.astype(bf16), z11.astype(bf16)
        gram[:B, :B] = z00 + nt(c00, p00)
        gram[B:, :B] = z10 + nt(c10, p00)
        gram[B:, B:] = z11 + (nt(c10, p10) + nt(c11, p11))
        w[:B, :B] += nn(p00, w0)
        w[B:, :B] += nn(p10, w0) + nn(p11, w1[:, :B])
        w[B:, B:] += nn(p11, w1[:, B:])
        return carry

    def fine(_, carry):
        w0h, w0l = split(w[:B, :B])
        w1h, w1l = split(w[B:, :])
        y0h, y0l = split(nn3(w0h, w0l, ah[:B, :B], al[:B, :B]))
        y1h, y1l = split(nn3(w1h, w1l, ah[...], al[...]))
        apply(
            w0h, w1h, nt3(y0h, y0l, w0h, w0l), nt3(y1h[:, :B], y1l[:, :B], w0h, w0l), nt3(y1h, y1l, w1h, w1l)
        )
        return carry

    lax.fori_loop(0, COARSE, coarse, 0)
    lax.fori_loop(0, FINE, fine, 0)
    wh[...], wl[...] = split(w[...] * scale_cols)

    def begin(which):
        scatter(which, 0).wait_recv()
        for copy in line_hops(which).values():
            copy.start()
        for copy in ring_hops(which, (0,), (0,)):
            copy.start()

    def feed_near(which):
        for step in (1, 3):
            line_hops(which)[step].wait_recv()
        for copy in ring_hops(which, (1, 3), (3, 1)):
            copy.start()

    def feed_far(which):
        line_hops(which)[2].wait_recv()
        for copy in ring_hops(which, (2,), (2,)):
            copy.start()

    def pass_on(which):
        for copy in ring_hops(which, (0, 1), (0, 3, 2)):
            copy.wait_recv()
        for copy in ring_hops(which, (4, 5), (4, 5)):
            copy.start()
        for copy in ring_hops(which, (3, 2), (1,)):
            copy.wait_recv()

    begin(0)
    begin(1)
    fetch_slab.start()
    fetch_panel.wait()
    fetch_mask.wait()

    def solve(left_part, right_part):
        lh, ll = split(left_part)
        qh, ql = split(right_part)
        first = nt3(lh, ll, wh[:B, :B], wl[:B, :B])
        second = nt3(lh, ll, wh[B:, :B], wl[B:, :B]) + nt3(qh, ql, wh[B:, B:], wl[B:, B:])
        return first, second

    def marked(ref, start, size, first_block):
        halves = []
        for k in range(2):
            parts = [
                ref[rows_at(start + at, B), k * B:(k + 1) * B] * mask[k, first_block + at // B].astype(f32)
                for at in range(0, size, B)
            ]
            halves.append(jnp.concatenate(parts, axis=0))
        return halves

    panes = mine.shape[0] // PANE

    def solve_mine(t, carry):
        part = rows_at(t * PANE, PANE)
        parts = solve(*marked(mine, t * PANE, PANE, (row * panes + t) * (PANE // B)))
        for at, value in zip((0, B), parts):
            mine[part, at:at + B] = value
            rh[part, at:at + B], rl[part, at:at + B] = split(value)
        return carry

    lax.fori_loop(0, panes // 2, solve_mine, 0, unroll=True)
    feed_near(0)
    feed_far(0)
    lax.fori_loop(panes // 2, 3 * panes // 4, solve_mine, 0, unroll=True)
    feed_near(1)
    lax.fori_loop(3 * panes // 4, panes, solve_mine, 0, unroll=True)
    feed_far(1)

    def masked_need(which, step):
        start = half * which + (((z, x)[which] + step) % 4) * wide
        part = rows_at(start, wide)
        block = col * (2 * half // B) + start // B
        left_part = need[part, :B] * mask[0, block].astype(f32)
        right_part = need[part, B:] * mask[1, block].astype(f32)
        return pl.ds(pl.multiple_of(start, 128), wide), left_part, right_part

    peak[...] = jnp.zeros_like(peak)

    def update(one, two):
        at0, left0, right0 = masked_need(*one)
        at1, left1, right1 = masked_need(*two)
        first, second = solve(jnp.concatenate([left0, left1], axis=0), jnp.concatenate([right0, right1], axis=0))
        gh[:, :B], gl[:, :B] = split(first)
        gh[:, B:], gl[:, B:] = split(second)

        def update_rows(t, carry):
            part = rows_at(t * TALL, TALL)
            product = nt3(rh[part, :], rl[part, :], gh[...], gl[...])
            for at, value in ((at0, product[:, :wide]), (at1, product[:, wide:])):
                value = slab[part, at] - value
                slab[part, at] = value
                size = jnp.max(jnp.abs(value).reshape(-1, 8, wide), axis=0)
                peak[...] = jnp.maximum(peak[...], size)
            return carry

        lax.fori_loop(0, mine.shape[0] // TALL, update_rows, 0, unroll=UNROLL)

    fetch_slab.wait()
    update((0, 0), (1, 0))
    pass_on(0)
    update((0, 1), (0, 3))
    pass_on(1)
    update((1, 1), (1, 3))
    for which in range(2):
        for copy in ring_hops(which, (4, 5), (4, 5)):
            copy.wait_recv()
    update((0, 2), (1, 2))

    def share(src, dst, sems, d, device):
        return pltpu.make_async_remote_copy(
            src_ref=src, dst_ref=dst.at[d - 1], send_sem=sems[0].at[d - 1], recv_sem=sems[1].at[d - 1],
            device_id=device, device_id_type=MESH,
        )

    def share_cols(d):
        return share(told.at[0], cols_in, (col_send, col_recv), d, (row, (col + d) % cols))

    def share_rows(d):
        return share(told.at[1], rows_in, (row_send, row_recv), d, ((row + d) % rows, col))

    best = jnp.max(peak[...], axis=0, keepdims=True)
    told[0] = best
    for d in far_first(cols):
        share_cols(d).start()
    for d in range(1, cols):
        share_cols(d).wait_recv()
    for d in range(1, cols):
        best = jnp.maximum(best, cols_in[d - 1])
    told[1] = best
    for d in far_first(rows):
        share_rows(d).start()

    for which in range(2):
        for copy in line_hops(which).values():
            copy.wait_send()
        for copy in ring_hops(which, range(6), range(6)):
            copy.wait_send()

    @pl.when(is_source)
    def _():
        for which in range(2):
            for step in range(4):
                scatter(which, step).wait_send()

    for d in range(1, cols):
        share_cols(d).wait_send()
    for d in range(1, rows):
        share_rows(d).wait_recv()
    for d in range(1, rows):
        best = jnp.maximum(best, rows_in[d - 1])
    growth_ref[0, 0] = jnp.max(best)
    for d in range(1, rows):
        share_rows(d).wait_send()


def store_kernel(rows_ref, slab_ref, rows_out, slab_out, sems):
    copies = []
    for src, dst in ((slab_ref, slab_out), (rows_ref, rows_out)):
        for at in range(0, src.shape[0], CHUNK):
            part = pl.ds(at, CHUNK)
            copies.append(pltpu.make_async_copy(src.at[part], dst.at[part], sems.at[len(copies)]))
    for copy in copies:
        copy.start()
    for copy in copies:
        copy.wait()


def body(diag_block, panel, block_mask, slab):
    rows_dev, cols_dev = slab.shape
    n_rows, n_cols = lax.axis_size("row"), lax.axis_size("col")
    vmem = pl.BlockSpec(memory_space=pltpu.VMEM)
    smem = pl.BlockSpec(memory_space=pltpu.SMEM)
    hbm = pl.BlockSpec(memory_space=pltpu.HBM)
    dma = pltpu.SemaphoreType.DMA
    marks = block_mask.T
    rows, updated, growth = pl.pallas_call(
        front_kernel,
        out_shape=(
            jax.ShapeDtypeStruct((rows_dev, PW), f32),
            jax.ShapeDtypeStruct((rows_dev, cols_dev), f32),
            jax.ShapeDtypeStruct((1, 1), f32),
        ),
        in_specs=[hbm, hbm, hbm, hbm],
        out_specs=(vmem, vmem, smem),
        scratch_shapes=[
            pltpu.VMEM((PW, PW), f32),
            pltpu.SMEM(marks.shape, jnp.int32),
            pltpu.VMEM((PW, PW), f32),
            pltpu.VMEM((PW, PW), bf16),
            pltpu.VMEM((PW, PW), bf16),
            pltpu.VMEM((PW, PW), f32),
            pltpu.VMEM((PW, PW), bf16),
            pltpu.VMEM((PW, PW), bf16),
            pltpu.VMEM((rows_dev, PW), bf16),
            pltpu.VMEM((rows_dev, PW), bf16),
            pltpu.VMEM((B, PW), bf16),
            pltpu.VMEM((B, PW), bf16),
            pltpu.VMEM((cols_dev, PW), f32),
            pltpu.VMEM((8, 128), f32),
            pltpu.VMEM((2, 1, 128), f32),
            pltpu.VMEM((n_cols - 1, 1, 128), f32),
            pltpu.VMEM((n_rows - 1, 1, 128), f32),
            dma,
            dma,
            dma,
            dma,
            dma((8,)),
            dma((2,)),
            dma((6,)),
            dma((6,)),
            dma((24,)),
            dma((24,)),
            dma((n_cols - 1,)),
            dma((n_cols - 1,)),
            dma((n_rows - 1,)),
            dma((n_rows - 1,)),
        ],
        compiler_params=pltpu.CompilerParams(
            collective_id=0, has_side_effects=True, vmem_limit_bytes=32 << 20
        ),
        name="front",
    )(*(pltpu.with_memory_space_constraint(a, pltpu.HBM) for a in (diag_block, marks, panel, slab)))

    out_rows, out_slab = pl.pallas_call(
        store_kernel,
        out_shape=(
            jax.ShapeDtypeStruct((rows_dev, PW), f32),
            jax.ShapeDtypeStruct((rows_dev, cols_dev), f32),
        ),
        in_specs=[vmem, vmem],
        out_specs=(hbm, hbm),
        scratch_shapes=[dma((2 * rows_dev // CHUNK,))],
        compiler_params=pltpu.CompilerParams(vmem_limit_bytes=1 << 20),
        name="store",
    )(rows, updated)
    return (out_rows, out_slab, growth.reshape(()))


def solution(mesh):
    in_specs = (P(), P("row", None), P(), P("row", "col"))
    out_specs = (P("row", None), P("row", "col"), P())
    return jax.shard_map(body, mesh=mesh, in_specs=in_specs, out_specs=out_specs, check_vma=False)
```

```python
import jax
import jax.numpy as jnp
from jax import lax
from jax.experimental import pallas as pl
from jax.experimental.pallas import tpu as pltpu
from jax.sharding import PartitionSpec as P

B = 256
PW = 512
COARSE = 7
FINE = 2
TALL = 512
CHUNK = 512
UNROLL = 4
PANE = 512
PASSED = {1: (0, 1), -1: (3, 2)}
MESH = pl.DeviceIdType.MESH
f32 = jnp.float32
bf16 = jnp.bfloat16


def nn(a, b):
    return lax.dot_general(a, b, (((1,), (0,)), ((), ())), preferred_element_type=f32)


def nt(a, b):
    return lax.dot_general(a, b, (((1,), (1,)), ((), ())), preferred_element_type=f32)


def split(a):
    high = a.astype(bf16)
    return high, (a - high.astype(f32)).astype(bf16)


def nt3(ah, al, bh, bl):
    return nt(ah, bh) + (nt(ah, bl) + nt(al, bh))


def nn3(ah, al, bh, bl):
    return nn(ah, bh) + (nn(ah, bl) + nn(al, bh))


def rows_at(start, size):
    return pl.ds(pl.multiple_of(start, 16), size)


def far_first(size):
    return sorted(range(1, size), key=lambda d: -min(d, size - d))


def front_kernel(
    diag_hbm, mask_hbm, panel_hbm, slab_hbm, mine, slab, growth_ref,
    diag, mask, gram, ah, al, w, wh, wl, rh, rl, gh, gl, need, peak, told, cols_in, rows_in,
    diag_sem, mask_sem, panel_sem, slab_sem, out_sem, in_sem, line_send, line_recv, ring_send, ring_recv,
    col_send, col_recv, row_send, row_recv,
):
    row, col = lax.axis_index("row"), lax.axis_index("col")
    z, x = row // 4, row % 4
    y, core = col // 2, col % 2
    half = need.shape[0] // 2
    piece = half // 16
    wide = 4 * piece
    rows, cols = lax.axis_size("row"), lax.axis_size("col")

    is_source = row < 4
    source = (y, ((y + 2 + z) % 4) * 2 + core)
    target_z = (y - row + 18) % 4

    def along_x(step):
        return z * 4 + (x + step) % 4

    def along_z(step):
        return ((z + step) % 4) * 4 + x

    fetch_diag = pltpu.make_async_copy(diag_hbm, diag, diag_sem)
    fetch_mask = pltpu.make_async_copy(mask_hbm, mask, mask_sem)
    fetch_panel = pltpu.make_async_copy(panel_hbm, mine, panel_sem)
    fetch_slab = pltpu.make_async_copy(slab_hbm, slab, slab_sem)
    fetch_diag.start()
    fetch_mask.start()

    barrier = pltpu.get_barrier_semaphore()

    def greet(device):
        pl.semaphore_signal(barrier, inc=1, device_id=device, device_id_type=MESH)

    greet(source)

    @pl.when(is_source)
    def _():
        for step in range(4):
            greet((target_z * 4 + (row + step) % 4, row * 2 + core))

    for step in range(1, 4):
        greet((along_x(step), col))
        greet((along_z(step), col))
    for d in range(1, cols):
        greet((row, (col + d) % cols))

    @pl.when(is_source)
    def _():
        pl.semaphore_wait(barrier, 10 + cols)

    def spot(which, dz, dx):
        if which == 0:
            return (dz * 4 + dx) * piece
        return half + (dx * 4 + dz) * piece

    def scatter(which, step):
        dx = (row + step) % 4
        start = spot(which, target_z, dx)
        return pltpu.make_async_remote_copy(
            src_ref=panel_hbm.at[rows_at(core * 2 * half + start, piece)], dst_ref=need.at[rows_at(start, piece)],
            send_sem=out_sem.at[which * 4 + step], recv_sem=in_sem.at[which],
            device_id=(target_z * 4 + dx, row * 2 + core), device_id_type=MESH,
        )

    @pl.when(is_source)
    def _():
        for which in range(2):
            for step in (2, 1, 3, 0):
                scatter(which, step).start()

    fetch_panel.start()

    def hop(sems, index, start, size, device):
        part = need.at[rows_at(start, size)]
        return pltpu.make_async_remote_copy(
            src_ref=part, dst_ref=part, send_sem=sems[0].at[index], recv_sem=sems[1].at[index],
            device_id=(device, col), device_id_type=MESH,
        )

    line, ring = (line_send, line_recv), (ring_send, ring_recv)

    def line_hops(which):
        along = (along_x, along_z)[which]
        return {step: hop(line, 3 * which + step - 1, spot(which, z, x), piece, along(step)) for step in (2, 1, 3)}

    def ring_hop(which, sign, index):
        at, fine_at, along = ((z, x, along_z), (x, z, along_x))[which]
        owner, offset = (at, index) if index < 4 else ((at + 4 - sign) % 4, PASSED[sign][index - 4])
        start = half * which + owner * wide + ((fine_at + offset) % 4) * piece
        return hop(ring, which * 12 + (0 if sign == 1 else 6) + index, start, piece, along(sign % 4))

    def ring_hops(which, plus, minus):
        for k in range(max(len(plus), len(minus))):
            for sign, indices in ((1, plus), (-1, minus)):
                if k < len(indices):
                    yield ring_hop(which, sign, indices[k])

    fetch_diag.wait()
    a = diag[...]
    r_id = lax.broadcasted_iota(jnp.int32, (PW, PW), 0)
    c_id = lax.broadcasted_iota(jnp.int32, (PW, PW), 1)
    on_diag = jnp.where(r_id == c_id, a, 0.0)
    scale_rows = lax.rsqrt(jnp.sum(on_diag, axis=1, keepdims=True))
    scale_cols = lax.rsqrt(jnp.sum(on_diag, axis=0, keepdims=True))
    scaled = a * scale_rows * scale_cols
    ah[...], al[...] = split(scaled)
    w[...] = jnp.where(r_id == c_id, 1.0, 0.0)
    gram[...] = scaled

    rb = lax.broadcasted_iota(jnp.int32, (B, B), 0)
    cb = lax.broadcasted_iota(jnp.int32, (B, B), 1)

    def correction(gram):
        return jnp.where(rb == cb, 0.5 - 0.5 * gram, jnp.where(rb > cb, -gram, 0.0)).astype(bf16)

    def apply(w0, w1, x00, x10, x11):
        p00, p10, p11 = correction(x00), (-x10).astype(bf16), correction(x11)
        w[:B, :B] += nn(p00, w0)
        w[B:, :B] += nn(p10, w0) + nn(p11, w1[:, :B])
        w[B:, B:] += nn(p11, w1[:, B:])

    def coarse(_, carry):
        g00, g10, g11 = gram[:B, :B], gram[B:, :B], gram[B:, B:]
        w0, w1 = w[:B, :B].astype(bf16), w[B:, :].astype(bf16)
        p00, p10, p11 = correction(g00), (-g10).astype(bf16), correction(g11)
        b00, b10, b11 = g00.astype(bf16), g10.astype(bf16), g11.astype(bf16)
        z00 = g00 + nn(p00, b00)
        z10 = g10 + (nn(p10, b00) + nn(p11, b10))
        z11 = g11 + (nt(p10, b10) + nn(p11, b11))
        c00, c10, c11 = z00.astype(bf16), z10.astype(bf16), z11.astype(bf16)
        gram[:B, :B] = z00 + nt(c00, p00)
        gram[B:, :B] = z10 + nt(c10, p00)
        gram[B:, B:] = z11 + (nt(c10, p10) + nt(c11, p11))
        w[:B, :B] += nn(p00, w0)
        w[B:, :B] += nn(p10, w0) + nn(p11, w1[:, :B])
        w[B:, B:] += nn(p11, w1[:, B:])
        return carry

    def fine(_, carry):
        w0h, w0l = split(w[:B, :B])
        w1h, w1l = split(w[B:, :])
        y0h, y0l = split(nn3(w0h, w0l, ah[:B, :B], al[:B, :B]))
        y1h, y1l = split(nn3(w1h, w1l, ah[...], al[...]))
        apply(
            w0h, w1h, nt3(y0h, y0l, w0h, w0l), nt3(y1h[:, :B], y1l[:, :B], w0h, w0l), nt3(y1h, y1l, w1h, w1l)
        )
        return carry

    lax.fori_loop(0, COARSE, coarse, 0)
    lax.fori_loop(0, FINE, fine, 0)
    wh[...], wl[...] = split(w[...] * scale_cols)

    @pl.when(jnp.logical_not(is_source))
    def _():
        pl.semaphore_wait(barrier, 6 + cols)

    def begin(which):
        scatter(which, 0).wait_recv()
        for copy in line_hops(which).values():
            copy.start()
        for copy in ring_hops(which, (0,), (0,)):
            copy.start()

    def feed_near(which):
        for step in (1, 3):
            line_hops(which)[step].wait_recv()
        for copy in ring_hops(which, (1, 3), (3, 1)):
            copy.start()

    def feed_far(which):
        line_hops(which)[2].wait_recv()
        for copy in ring_hops(which, (2,), (2,)):
            copy.start()

    def pass_on(which):
        for copy in ring_hops(which, (0, 1), (0, 3, 2)):
            copy.wait_recv()
        for copy in ring_hops(which, (4, 5), (4, 5)):
            copy.start()
        for copy in ring_hops(which, (3, 2), (1,)):
            copy.wait_recv()

    begin(0)
    begin(1)
    fetch_slab.start()
    fetch_panel.wait()
    fetch_mask.wait()

    def solve(left_part, right_part):
        lh, ll = split(left_part)
        qh, ql = split(right_part)
        first = nt3(lh, ll, wh[:B, :B], wl[:B, :B])
        second = nt3(lh, ll, wh[B:, :B], wl[B:, :B]) + nt3(qh, ql, wh[B:, B:], wl[B:, B:])
        return first, second

    def marked(ref, start, size, first_block):
        halves = []
        for k in range(2):
            parts = [
                ref[rows_at(start + at, B), k * B:(k + 1) * B] * mask[k, first_block + at // B].astype(f32)
                for at in range(0, size, B)
            ]
            halves.append(jnp.concatenate(parts, axis=0))
        return halves

    panes = mine.shape[0] // PANE

    def solve_mine(t, carry):
        part = rows_at(t * PANE, PANE)
        parts = solve(*marked(mine, t * PANE, PANE, (row * panes + t) * (PANE // B)))
        for at, value in zip((0, B), parts):
            mine[part, at:at + B] = value
            rh[part, at:at + B], rl[part, at:at + B] = split(value)
        return carry

    lax.fori_loop(0, panes // 2, solve_mine, 0, unroll=True)
    feed_near(0)
    feed_far(0)
    lax.fori_loop(panes // 2, 3 * panes // 4, solve_mine, 0, unroll=True)
    feed_near(1)
    lax.fori_loop(3 * panes // 4, panes, solve_mine, 0, unroll=True)
    feed_far(1)

    def masked_need(which, step):
        start = half * which + (((z, x)[which] + step) % 4) * wide
        part = rows_at(start, wide)
        block = col * (2 * half // B) + start // B
        left_part = need[part, :B] * mask[0, block].astype(f32)
        right_part = need[part, B:] * mask[1, block].astype(f32)
        return pl.ds(pl.multiple_of(start, 128), wide), left_part, right_part

    peak[...] = jnp.zeros_like(peak)

    def update(one, two):
        at0, left0, right0 = masked_need(*one)
        at1, left1, right1 = masked_need(*two)
        first, second = solve(jnp.concatenate([left0, left1], axis=0), jnp.concatenate([right0, right1], axis=0))
        gh[:, :B], gl[:, :B] = split(first)
        gh[:, B:], gl[:, B:] = split(second)

        def update_rows(t, carry):
            part = rows_at(t * TALL, TALL)
            product = nt3(rh[part, :], rl[part, :], gh[...], gl[...])
            for at, value in ((at0, product[:, :wide]), (at1, product[:, wide:])):
                value = slab[part, at] - value
                slab[part, at] = value
                size = jnp.max(jnp.abs(value).reshape(-1, 8, wide), axis=0)
                peak[...] = jnp.maximum(peak[...], size)
            return carry

        lax.fori_loop(0, mine.shape[0] // TALL, update_rows, 0, unroll=UNROLL)

    fetch_slab.wait()
    update((0, 0), (1, 0))
    pass_on(0)
    update((0, 1), (0, 3))
    pass_on(1)
    update((1, 1), (1, 3))
    for which in range(2):
        for copy in ring_hops(which, (4, 5), (4, 5)):
            copy.wait_recv()
    update((0, 2), (1, 2))

    def share(src, dst, sems, d, device):
        return pltpu.make_async_remote_copy(
            src_ref=src, dst_ref=dst.at[d - 1], send_sem=sems[0].at[d - 1], recv_sem=sems[1].at[d - 1],
            device_id=device, device_id_type=MESH,
        )

    def share_cols(d):
        return share(told.at[0], cols_in, (col_send, col_recv), d, (row, (col + d) % cols))

    def share_rows(d):
        return share(told.at[1], rows_in, (row_send, row_recv), d, ((row + d) % rows, col))

    best = jnp.max(peak[...], axis=0, keepdims=True)
    told[0] = best
    for d in far_first(cols):
        share_cols(d).start()
    for d in range(1, cols):
        share_cols(d).wait_recv()
    for d in range(1, cols):
        best = jnp.maximum(best, cols_in[d - 1])
    told[1] = best
    for d in far_first(rows):
        share_rows(d).start()

    for which in range(2):
        for copy in line_hops(which).values():
            copy.wait_send()
        for copy in ring_hops(which, range(6), range(6)):
            copy.wait_send()

    @pl.when(is_source)
    def _():
        for which in range(2):
            for step in range(4):
                scatter(which, step).wait_send()

    for d in range(1, cols):
        share_cols(d).wait_send()
    for d in range(1, rows):
        share_rows(d).wait_recv()
    for d in range(1, rows):
        best = jnp.maximum(best, rows_in[d - 1])
    growth_ref[0, 0] = jnp.max(best)
    for d in range(1, rows):
        share_rows(d).wait_send()


def store_kernel(rows_ref, slab_ref, rows_out, slab_out, sems):
    copies = []
    for src, dst in ((slab_ref, slab_out), (rows_ref, rows_out)):
        for at in range(0, src.shape[0], CHUNK):
            part = pl.ds(at, CHUNK)
            copies.append(pltpu.make_async_copy(src.at[part], dst.at[part], sems.at[len(copies)]))
    for copy in copies:
        copy.start()
    for copy in copies:
        copy.wait()


def body(diag_block, panel, block_mask, slab):
    rows_dev, cols_dev = slab.shape
    n_rows, n_cols = lax.axis_size("row"), lax.axis_size("col")
    vmem = pl.BlockSpec(memory_space=pltpu.VMEM)
    smem = pl.BlockSpec(memory_space=pltpu.SMEM)
    hbm = pl.BlockSpec(memory_space=pltpu.HBM)
    dma = pltpu.SemaphoreType.DMA
    marks = block_mask.T
    rows, updated, growth = pl.pallas_call(
        front_kernel,
        out_shape=(
            jax.ShapeDtypeStruct((rows_dev, PW), f32),
            jax.ShapeDtypeStruct((rows_dev, cols_dev), f32),
            jax.ShapeDtypeStruct((1, 1), f32),
        ),
        in_specs=[hbm, hbm, hbm, hbm],
        out_specs=(vmem, vmem, smem),
        scratch_shapes=[
            pltpu.VMEM((PW, PW), f32),
            pltpu.SMEM(marks.shape, jnp.int32),
            pltpu.VMEM((PW, PW), f32),
            pltpu.VMEM((PW, PW), bf16),
            pltpu.VMEM((PW, PW), bf16),
            pltpu.VMEM((PW, PW), f32),
            pltpu.VMEM((PW, PW), bf16),
            pltpu.VMEM((PW, PW), bf16),
            pltpu.VMEM((rows_dev, PW), bf16),
            pltpu.VMEM((rows_dev, PW), bf16),
            pltpu.VMEM((B, PW), bf16),
            pltpu.VMEM((B, PW), bf16),
            pltpu.VMEM((cols_dev, PW), f32),
            pltpu.VMEM((8, 128), f32),
            pltpu.VMEM((2, 1, 128), f32),
            pltpu.VMEM((n_cols - 1, 1, 128), f32),
            pltpu.VMEM((n_rows - 1, 1, 128), f32),
            dma,
            dma,
            dma,
            dma,
            dma((8,)),
            dma((2,)),
            dma((6,)),
            dma((6,)),
            dma((24,)),
            dma((24,)),
            dma((n_cols - 1,)),
            dma((n_cols - 1,)),
            dma((n_rows - 1,)),
            dma((n_rows - 1,)),
        ],
        compiler_params=pltpu.CompilerParams(
            collective_id=0, has_side_effects=True, vmem_limit_bytes=32 << 20
        ),
        name="front",
    )(*(pltpu.with_memory_space_constraint(a, pltpu.HBM) for a in (diag_block, marks, panel, slab)))

    out_rows, out_slab = pl.pallas_call(
        store_kernel,
        out_shape=(
            jax.ShapeDtypeStruct((rows_dev, PW), f32),
            jax.ShapeDtypeStruct((rows_dev, cols_dev), f32),
        ),
        in_specs=[vmem, vmem],
        out_specs=(hbm, hbm),
        scratch_shapes=[dma((2 * rows_dev // CHUNK,))],
        compiler_params=pltpu.CompilerParams(vmem_limit_bytes=1 << 20),
        name="store",
    )(rows, updated)
    return (out_rows, out_slab, growth.reshape(()))


def solution(mesh):
    in_specs = (P(), P("row", None), P(), P("row", "col"))
    out_specs = (P("row", None), P("row", "col"), P())
    return jax.shard_map(body, mesh=mesh, in_specs=in_specs, out_specs=out_specs, check_vma=False)
```
